512 devices in a mesh: src: 16 (over z_lo, x), tgt: 4 (over z_hi), feat: 8 (over y, core).
Axes of the slice: x: 4, y: 4, z: 16 (z_hi: 4, z_lo: 4; z = z_hi * 4 + z_lo), core: 2. Of those that a mesh axis runs over, the one named last changes fastest.
Arguments:
- activations: bfloat16 [16, 1792, 1280], P('src', None, 'feat'), may hold values from 0 to 12, as said below
- window_ids: int32 [16, 640], replicated, may hold values from 0 to 1279, as said below
- decoders: bfloat16 [16, 16, 640, 2048], P('src', 'tgt', 'feat'), may hold values from -3 to 3
- encoders: bfloat16 [16, 2048, 640], P('tgt', ('src', 'feat')), may hold values from -0.125 to 0.125
Outputs:
- weighted: float32 [16, 16, 640, 640], P('src', 'tgt', 'feat')
The draws below stay inside these ranges and needn't reach their ends.
Inputs may be any that keep to these rules, and one draw needn't show every extreme that they name: `window_ids`: each layer's list names 640 distinct features. activations are zero or positive.
All inputs are finite; a program needn't handle non-finite values.
Results may differ from the reference program's by a relative error of at most 0.0029.
Values may be sent and summed in bfloat16 or wider, within the bound.
No kernel may reach another device: no remote copies, remote signals or barrier semaphores. Data moves between devices by JAX's collectives and lax.ppermute only.
A program may use at most 64 MiB of HBM per device.

```python
import jax
import jax.numpy as jnp
from jax import lax

D = 2048
FEATS = 1280
FW = 640
TOKENS = 1792
LAYERS = 16


def draw_activations(key, part):
    chosen_entry_filter, key_tier = jax.random.split(key, 2)
    full_dimensions = (LAYERS, TOKENS, FEATS)
    active_flag = (jax.random.randint(chosen_entry_filter, full_dimensions, 0, 4) == 0).astype(jnp.float32)
    per_depth_results = jnp.exp(jax.random.uniform(key_tier, full_dimensions, jnp.float32, jnp.log(0.5), jnp.log(6.0)))
    return (active_flag * per_depth_results).astype(jnp.bfloat16)


def draw_window_ids(key, part):

    def one_layer(layer_key):
        key_pick, key_order = jax.random.split(layer_key)
        middle_ids = (jax.random.permutation(key_pick, FEATS - 2)[:FW - 2] + 1).astype(jnp.int32)
        listed = jnp.concatenate([jnp.array([0, FEATS - 1], jnp.int32), middle_ids])
        return listed[jax.random.permutation(key_order, FW)]
    return jax.vmap(one_layer)(jax.random.split(jax.random.fold_in(key, 7), LAYERS))


def block_levels(own_key, extent, cuts, least, high):
    def one(axis_at, parts):
        steps = jax.random.uniform(jax.random.fold_in(jax.random.fold_in(own_key, 6), axis_at), (parts,), jnp.float32, least / len(cuts), high / len(cuts))
        return jnp.repeat(jnp.exp(steps), extent[axis_at] // parts).reshape((-1,) + (1,) * (len(extent) - axis_at - 1))

    level = one(*cuts[0])
    for cut in cuts[1:]:
        level = level * one(*cut)
    return level


def centred(own_key, shape, spread, limit, shards=(), held_as=jnp.bfloat16):
    entries = jax.random.normal(own_key, shape, jnp.float32) * spread
    if len(shards) > 0:
        entries = block_levels(own_key, shape, shards, -0.22, 0.18) * entries
    return jnp.clip(entries, min=-limit, max=limit).astype(held_as)


def setup_inputs(seed: int = 0) -> dict:
    streams_of = jax.random.split(jax.random.key(seed), 5)
    activations = draw_activations(jax.random.fold_in(streams_of[4], 71), 0)
    window_ids = draw_window_ids(jax.random.fold_in(streams_of[4], 71), 0)
    decoders = centred(streams_of[2], (LAYERS, LAYERS, FW, D), 0.5, 3.0, ((0, 16), (1, 4), (2, 8)))
    encoders = centred(streams_of[3], (LAYERS, D, FW), D ** -0.5, 0.125, ((0, 4), (1, 128)))
    return dict(activations=activations, window_ids=window_ids, decoders=decoders, encoders=encoders)


def reference(activations, window_ids, decoders, encoders):
    windows = jax.vmap(lambda acts_layer, ids_layer: jnp.take(acts_layer, ids_layer, axis=1))(activations, window_ids)
    windows_wide = windows.astype(jnp.float32)
    encoders_wide = encoders.astype(jnp.float32)
    depth_numbers = jnp.arange(LAYERS).astype(jnp.int32)

    def one_source(source):
        written = lax.dynamic_index_in_dim(decoders, source, 0, keepdims=False).astype(jnp.float32)
        live_mask = (depth_numbers >= source).astype(jnp.float32)
        written = written * live_mask[:, None, None]
        running = jnp.cumsum(written, 0)
        leading_sum = jnp.concatenate([jnp.zeros_like(running[:1]), running[:-1]], 0).astype(jnp.bfloat16)
        virtual = jnp.einsum("tid,tdj->tij", leading_sum.astype(jnp.float32), encoders_wide, precision=lax.Precision.HIGHEST)
        source_window = lax.dynamic_index_in_dim(windows_wide, source, 0, keepdims=False)
        gram = jnp.einsum("ni,tnj->tij", source_window, windows_wide, precision=lax.Precision.HIGHEST) / TOKENS
        return virtual * gram

    return lax.map(one_source, depth_numbers)
```

```python
import jax
import jax.numpy as jnp
from jax import lax
from jax.experimental import pallas as pl
from jax.experimental.pallas import tpu as pltpu
from jax.sharding import Mesh, PartitionSpec as P

ZLO, X, TGT, Y, CORE = 4, 4, 4, 4, 2
FEAT = ("y", "core")


def total_pairs(k):
    return [(z * TGT + b, z * TGT + b + k) for z in range(ZLO) for b in range(z, TGT - k)]


def window_pairs(k):
    return [(b * TGT + b, (b - k) * TGT + b) for b in range(k, TGT)]


def finish_kernel(gathered_ref, prefix_ref, window_ref, out_ref):
    slices, rows, width = gathered_ref.shape
    sources, height, tokens = window_ref.shape[0], window_ref.shape[2], window_ref.shape[3]
    groups = (rows - tokens) // 16
    chunk = slices * 16
    gram = jnp.zeros((sources * height, width), jnp.float32)
    for f in range(slices):
        own = window_ref[:, f].reshape(sources * height, tokens)
        gram += jnp.dot(own, gathered_ref[f, :tokens], preferred_element_type=jnp.float32)
    virtual = jnp.zeros((sources * height, width), jnp.float32)
    for g in range(groups):
        left = prefix_ref[:, :, g * chunk : (g + 1) * chunk].reshape(sources * height, chunk)
        right = gathered_ref[:, tokens + 16 * g : tokens + 16 * (g + 1)].reshape(chunk, width)
        virtual += jnp.dot(left, right, preferred_element_type=jnp.float32)
    token_count = slices * tokens
    out_ref[...] = (virtual * (gram / token_count)).reshape(out_ref.shape)


def finish(gathered, prefix, window):
    return pl.pallas_call(
        finish_kernel,
        out_shape=jax.ShapeDtypeStruct((prefix.shape[0], prefix.shape[1], gathered.shape[2]), jnp.float32),
    )(gathered, prefix, window)


def per_device(activations, window_ids, decoders, encoders):
    zlo = lax.axis_index("zlo")
    block = lax.axis_index("tgt")
    source = zlo * X + lax.axis_index("x")
    token_count, local_feats = activations.shape[1:]
    targets, height = decoders.shape[1:3]
    fw = window_ids.shape[1]
    slices = Y * CORE
    tokens = token_count // slices

    depth = block * targets + jnp.arange(targets)
    live = (depth >= source).astype(jnp.float32)
    written = decoders[0].astype(jnp.float32) * live[:, None, None]
    before = [jnp.zeros_like(written[0])]
    for k in range(targets):
        before.append(before[-1] + written[k])
    total = before.pop()
    earlier = [lax.ppermute(total, ("zlo", "tgt"), total_pairs(k)) for k in (3, 2, 1)]

    by_tokens = activations[0].T.reshape(local_feats, slices, tokens).transpose(1, 0, 2)
    sliced = lax.all_to_all(by_tokens, FEAT, 0, 0, tiled=True).reshape(slices * local_feats, tokens)
    own_ids = lax.dynamic_index_in_dim(window_ids, source, 0, keepdims=False)
    chosen = (jnp.arange(slices * local_feats)[:, None] == own_ids[None, :]).astype(jnp.bfloat16)
    dims = (((0,), (0,)), ((), ()))
    columns = lax.dot_general(sliced, chosen, dims, preferred_element_type=jnp.float32).astype(jnp.bfloat16)
    rows = lax.dot_general(chosen, sliced, dims, preferred_element_type=jnp.float32).astype(jnp.bfloat16)

    parts = [lax.ppermute(columns, ("zlo", "tgt"), window_pairs(k)) for k in (3, 2, 1)]
    target = jnp.where(zlo == block, columns, parts[0] + parts[1] + parts[2])

    spread = jnp.broadcast_to(encoders[None], (ZLO,) + encoders.shape).reshape((ZLO * X,) + encoders.shape[1:])
    encoder_rows = lax.all_to_all(spread, ("zlo", "x"), 0, 0, tiled=True).reshape(-1, fw)
    gathered = lax.all_gather(jnp.concatenate([target, encoder_rows], 0), FEAT, axis=0)

    pieces = jnp.broadcast_to(rows.reshape(1, slices, height, tokens), (X, slices, height, tokens))
    pieces = pieces.reshape(X * slices, height, tokens)
    window = lax.all_to_all(pieces, ("x",) + FEAT, 0, 0, tiled=True).reshape(X, slices, height, tokens)

    base = earlier[0] + earlier[1] + earlier[2]
    prefix = jnp.stack([(base + part).astype(jnp.bfloat16) for part in before])
    prefix = lax.all_to_all(prefix, "x", 0, 0, tiled=True)

    weighted = finish(gathered, prefix, window)
    return lax.all_to_all(weighted, "x", 0, 0, tiled=True)[None]


def solution(mesh):
    fine = Mesh(mesh.devices.reshape(ZLO, X, TGT, Y, CORE), ("zlo", "x", "tgt", "y", "core"))
    src = ("zlo", "x")
    in_specs = (
        P(src, None, FEAT),
        P(),
        P(src, "tgt", FEAT, None),
        P("tgt", src + FEAT, None),
    )
    out_specs = P(src, "tgt", FEAT, None)
    return jax.shard_map(
        per_device, mesh=fine, in_specs=in_specs, out_specs=out_specs, check_vma=False
    )
```

```python
import jax
import jax.numpy as jnp
from jax import lax
from jax.experimental import pallas as pl
from jax.experimental.pallas import tpu as pltpu
from jax.sharding import Mesh, PartitionSpec as P

ZLO, X, TGT, Y, CORE = 4, 4, 4, 4, 2
FEAT = ("y", "core")


def total_pairs(k):
    return [(z * TGT + b, z * TGT + b + k) for z in range(ZLO) for b in range(z, TGT - k)]


def window_pairs(k):
    return [(b * TGT + b, (b - k) * TGT + b) for b in range(k, TGT)]


def virtual_kernel(place_ref, prefix_ref, own_ref, other_ref, out_ref, rows_ref):
    groups, slices, depth, width = rows_ref.shape
    core = place_ref[2]
    for r in range(Y):
        row = (place_ref[1] + Y - r) % Y
        rows_ref[:, row * CORE + core] = own_ref[r].reshape(groups, depth, width)
        rows_ref[:, row * CORE + 1 - core] = other_ref[r].reshape(groups, depth, width)
    height = prefix_ref.shape[0] * prefix_ref.shape[1]
    chunk = slices * depth
    total = jnp.zeros((height, width), jnp.float32)
    for g in range(groups):
        left = prefix_ref[:, :, g * chunk : (g + 1) * chunk].reshape(height, chunk)
        total += jnp.dot(left, rows_ref[g].reshape(chunk, width), preferred_element_type=jnp.float32)
    out_ref[...] = total.reshape(out_ref.shape)


def weigh_kernel(place_ref, virtual_ref, window_ref, own_ref, other_ref, out_ref):
    sources, slices, height, tokens = window_ref.shape
    x, core = place_ref[0], place_ref[2]
    width = own_ref.shape[2]
    order = [(x + X - r) % X for r in range(sources)]
    gram = jnp.zeros((sources * height, width), jnp.float32)
    for r in range(Y):
        row = (place_ref[1] + Y - r) % Y
        for piece, half in ((own_ref, core), (other_ref, 1 - core)):
            left = jnp.concatenate([window_ref[order[q], row * CORE + half] for q in range(sources)], 0)
            gram += jnp.dot(left, piece[r], preferred_element_type=jnp.float32)
    gram = gram / (slices * tokens)
    for q in range(sources):
        out_ref[order[q]] = virtual_ref[q] * gram[q * height : (q + 1) * height]


SMEM = pl.BlockSpec(memory_space=pltpu.SMEM)
VMEM = pl.BlockSpec(memory_space=pltpu.VMEM)


def virtual_of(place, prefix, own, other):
    sources, height, depth = prefix.shape
    width = own.shape[2]
    groups = ZLO * X
    return pl.pallas_call(
        virtual_kernel,
        out_shape=jax.ShapeDtypeStruct((sources, height, width), jnp.float32),
        in_specs=[SMEM, VMEM, VMEM, VMEM],
        out_specs=VMEM,
        scratch_shapes=[pltpu.VMEM((groups, Y * CORE, depth // (groups * Y * CORE), width), jnp.bfloat16)],
    )(place, prefix, own, other)


def weigh(place, virtual, window, own, other):
    return pl.pallas_call(
        weigh_kernel,
        out_shape=jax.ShapeDtypeStruct(virtual.shape, jnp.float32),
        in_specs=[SMEM, VMEM, VMEM, VMEM, VMEM],
        out_specs=VMEM,
    )(place, virtual, window, own, other)


def ring(n, k):
    return [(i, (i + k) % n) for i in range(n)]


def over_feat(piece):
    own = jnp.stack([piece] + [lax.ppermute(piece, "y", ring(Y, k)) for k in range(1, Y)])
    return own, lax.ppermute(own, "core", ring(CORE, 1))


def per_device(activations, window_ids, decoders, encoders):
    zlo = lax.axis_index("zlo")
    block = lax.axis_index("tgt")
    x = lax.axis_index("x")
    source = zlo * X + x
    token_count, local_feats = activations.shape[1:]
    targets, height = decoders.shape[1:3]
    fw = window_ids.shape[1]
    slices = Y * CORE
    tokens = token_count // slices

    depth = block * targets + jnp.arange(targets)
    live = (depth >= source).astype(jnp.float32)
    written = decoders[0].astype(jnp.float32) * live[:, None, None]
    before = [jnp.zeros_like(written[0])]
    for k in range(targets):
        before.append(before[-1] + written[k])
    total = before.pop()
    earlier = [lax.ppermute(total, ("zlo", "tgt"), total_pairs(k)) for k in (3, 2, 1)]

    by_tokens = activations[0].T.reshape(local_feats, slices, tokens).transpose(1, 0, 2)
    sliced = lax.all_to_all(by_tokens, FEAT, 0, 0, tiled=True).reshape(slices * local_feats, tokens)
    own_ids = lax.dynamic_index_in_dim(window_ids, source, 0, keepdims=False)
    chosen = (jnp.arange(slices * local_feats)[:, None] == own_ids[None, :]).astype(jnp.bfloat16)
    dims = (((0,), (0,)), ((), ()))
    columns = lax.dot_general(sliced, chosen, dims, preferred_element_type=jnp.float32).astype(jnp.bfloat16)
    rows = lax.dot_general(chosen, sliced, dims, preferred_element_type=jnp.float32).astype(jnp.bfloat16)

    parts = [lax.ppermute(columns, ("zlo", "tgt"), window_pairs(k)) for k in (3, 2, 1)]
    target = jnp.where(zlo == block, columns, parts[0] + parts[1] + parts[2])
    target_own, target_other = over_feat(target)

    spread = jnp.broadcast_to(encoders[None], (ZLO,) + encoders.shape).reshape((ZLO * X,) + encoders.shape[1:])
    encoder_rows = lax.all_to_all(spread, ("zlo", "x"), 0, 0, tiled=True).reshape(-1, fw)
    encoder_own, encoder_other = over_feat(encoder_rows)

    pieces = jnp.broadcast_to(rows.reshape(1, slices, height, tokens), (X, slices, height, tokens))
    pieces = pieces.reshape(X * slices, height, tokens)
    window = lax.all_to_all(pieces, ("x",) + FEAT, 0, 0, tiled=True).reshape(X, slices, height, tokens)

    base = earlier[0] + earlier[1] + earlier[2]
    prefix = jnp.stack([(base + part).astype(jnp.bfloat16) for part in before])
    pieces = [lax.dynamic_index_in_dim(prefix, (x + k) % X, 0, keepdims=False) for k in range(X)]
    prefix = jnp.stack([pieces[0]] + [lax.ppermute(pieces[k], "x", ring(X, k)) for k in range(1, X)])

    place = jnp.stack([x, lax.axis_index("y"), lax.axis_index("core")]).astype(jnp.int32)
    virtual = virtual_of(place, prefix, encoder_own, encoder_other)
    weighted = weigh(place, virtual, window, target_own, target_other)
    return lax.all_to_all(weighted, "x", 0, 0, tiled=True)[None]


def solution(mesh):
    fine = Mesh(mesh.devices.reshape(ZLO, X, TGT, Y, CORE), ("zlo", "x", "tgt", "y", "core"))
    src = ("zlo", "x")
    in_specs = (
        P(src, None, FEAT),
        P(),
        P(src, "tgt", FEAT, None),
        P("tgt", src + FEAT, None),
    )
    out_specs = P(src, "tgt", FEAT, None)
    return jax.shard_map(
        per_device, mesh=fine, in_specs=in_specs, out_specs=out_specs, check_vma=False
    )
```

```python
import jax
import jax.numpy as jnp
from jax import lax
from jax.experimental import pallas as pl
from jax.experimental.pallas import tpu as pltpu
from jax.sharding import Mesh, PartitionSpec as P

ZLO, X, TGT, Y, CORE = 4, 4, 4, 4, 2
FEAT = ("y", "core")


def total_pairs(k):
    return [(z * TGT + b, z * TGT + b + k) for z in range(ZLO) for b in range(z, TGT - k)]


def window_pairs(k):
    return [(b * TGT + b, (b - k) * TGT + b) for b in range(k, TGT)]


def split_kernel(wide_ref, out_ref):
    tokens = out_ref.shape[2]
    for f in range(out_ref.shape[0]):
        out_ref[f] = wide_ref[:, f * tokens : (f + 1) * tokens]


def select_kernel(place_ref, ids_ref, sliced_ref, columns_ref, pieces_ref):
    feats, tokens = sliced_ref.shape
    width = ids_ref.shape[1]
    step = 128
    row = ids_ref[pl.ds(place_ref[4], 1), :]
    wide = jnp.broadcast_to(row, (step, width))
    tall = wide.T
    columns = jnp.zeros((tokens, width), jnp.float32)
    rows = jnp.zeros((width, tokens), jnp.float32)
    for g in range(feats // step):
        part = sliced_ref[g * step : (g + 1) * step]
        chosen = (wide == g * step + lax.broadcasted_iota(jnp.int32, wide.shape, 0)).astype(jnp.bfloat16)
        columns += lax.dot_general(part, chosen, (((0,), (0,)), ((), ())), preferred_element_type=jnp.float32)
        chosen = (tall == g * step + lax.broadcasted_iota(jnp.int32, tall.shape, 1)).astype(jnp.bfloat16)
        rows += jnp.dot(chosen, part, preferred_element_type=jnp.float32)
    columns_ref[...] = columns.astype(columns_ref.dtype)
    rows = rows.astype(pieces_ref.dtype)
    height = width // (Y * CORE)
    for y in range(Y):
        for c in range(CORE):
            f = y * CORE + c
            for x in range(X):
                pieces_ref[x * CORE + c, y * height : (y + 1) * height] = rows[f * height : (f + 1) * height]


def virtual_kernel(place_ref, prefix_ref, own_ref, other_ref, out_ref, rows_ref):
    groups, slices, depth, width = rows_ref.shape
    core = place_ref[2]
    for r in range(Y):
        row = (place_ref[1] + Y - r) % Y
        rows_ref[:, row * CORE + core] = own_ref[r].reshape(groups, depth, width)
        rows_ref[:, row * CORE + 1 - core] = other_ref[r].reshape(groups, depth, width)
    height = prefix_ref.shape[0] * prefix_ref.shape[1]
    chunk = slices * depth
    total = jnp.zeros((height, width), jnp.float32)
    for g in range(groups):
        left = prefix_ref[:, :, g * chunk : (g + 1) * chunk].reshape(height, chunk)
        total += jnp.dot(left, rows_ref[g].reshape(chunk, width), preferred_element_type=jnp.float32)
    out_ref[...] = total.reshape(out_ref.shape)


def gram_kernel(place_ref, window_ref, own_ref, other_ref, out_ref):
    core = place_ref[2]
    for q in range(window_ref.shape[0]):
        part = jnp.dot(window_ref[q, core], own_ref[...], preferred_element_type=jnp.float32)
        part += jnp.dot(window_ref[q, 1 - core], other_ref[...], preferred_element_type=jnp.float32)
        out_ref[q] = part.astype(out_ref.dtype)


def weigh_kernel(place_ref, gram_ref, *refs):
    virtual_refs, out_ref = refs[:-1], refs[-1]
    token_count = place_ref[3].astype(jnp.float32)
    for r in range(X):
        layer = (place_ref[0] + r) % X
        gram = gram_ref[layer, 0].astype(jnp.float32)
        for row in range(1, Y):
            gram += gram_ref[layer, row].astype(jnp.float32)
        out_ref[layer] = virtual_refs[r][...] * (gram / token_count)


SMEM = pl.BlockSpec(memory_space=pltpu.SMEM)
VMEM = pl.BlockSpec(memory_space=pltpu.VMEM)


def split(wide, slices):
    feats, token_count = wide.shape
    return pl.pallas_call(
        split_kernel,
        out_shape=jax.ShapeDtypeStruct((slices, feats, token_count // slices), wide.dtype),
        in_specs=[VMEM],
        out_specs=VMEM,
    )(wide)


def select(place, window_ids, sliced):
    tokens, width = sliced.shape[1], window_ids.shape[1]
    return pl.pallas_call(
        select_kernel,
        out_shape=(
            jax.ShapeDtypeStruct((tokens, width), jnp.bfloat16),
            jax.ShapeDtypeStruct((X * CORE, width // CORE, tokens), jnp.bfloat16),
        ),
        in_specs=[SMEM, VMEM, VMEM],
        out_specs=(VMEM, VMEM),
    )(place, window_ids, sliced)


def virtual_of(place, prefix, own, other):
    sources, height, depth = prefix.shape
    width = own.shape[2]
    groups = ZLO * X
    return pl.pallas_call(
        virtual_kernel,
        out_shape=jax.ShapeDtypeStruct((sources, height, width), jnp.float32),
        in_specs=[SMEM, VMEM, VMEM, VMEM],
        out_specs=VMEM,
        scratch_shapes=[pltpu.VMEM((groups, Y * CORE, depth // (groups * Y * CORE), width), jnp.bfloat16)],
    )(place, prefix, own, other)


def gram_of(place, window, own, other):
    return pl.pallas_call(
        gram_kernel,
        out_shape=jax.ShapeDtypeStruct((X, window.shape[2], own.shape[1]), jnp.bfloat16),
        in_specs=[SMEM, VMEM, VMEM, VMEM],
        out_specs=VMEM,
    )(place, window, own, other)


def weigh(place, gram, virtual):
    return pl.pallas_call(
        weigh_kernel,
        out_shape=jax.ShapeDtypeStruct((X,) + virtual[0].shape, jnp.float32),
        in_specs=[SMEM, VMEM] + [VMEM] * len(virtual),
        out_specs=VMEM,
    )(place, gram, *virtual)


def ring(n, k):
    return [(i, (i + k) % n) for i in range(n)]


def over_feat(piece):
    others = [lax.ppermute(piece, "y", ring(Y, k)) for k in range(1, Y)]
    own = jnp.stack([piece] + others)
    return own, lax.ppermute(own, "core", ring(CORE, 1))


def per_device(activations, window_ids, decoders, encoders):
    zlo = lax.axis_index("zlo")
    block = lax.axis_index("tgt")
    x = lax.axis_index("x")
    source = zlo * X + x
    token_count, local_feats = activations.shape[1:]
    targets, height = decoders.shape[1:3]
    fw = window_ids.shape[1]
    slices = Y * CORE
    tokens = token_count // slices

    depth = block * targets + jnp.arange(targets)
    live = (depth >= source).astype(jnp.float32)
    written = decoders[0].astype(jnp.float32) * live[:, None, None]
    before = [jnp.zeros_like(written[0])]
    for k in range(targets):
        before.append(before[-1] + written[k])
    total = before.pop()
    earlier = [lax.ppermute(total, ("zlo", "tgt"), total_pairs(k)) for k in (3, 2, 1)]

    place = jnp.stack([x, lax.axis_index("y"), lax.axis_index("core"), token_count, source]).astype(jnp.int32)
    by_tokens = split(activations[0].T, slices)
    sliced = lax.all_to_all(by_tokens, FEAT, 0, 0, tiled=True).reshape(slices * local_feats, tokens)
    columns, pieces = select(place, window_ids, sliced)

    parts = [lax.ppermute(columns, ("zlo", "tgt"), window_pairs(k)) for k in (3, 2, 1)]
    target = jnp.where(zlo == block, columns, parts[0] + parts[1] + parts[2])
    swapped = lax.ppermute(target, "core", ring(CORE, 1))

    spread = jnp.broadcast_to(encoders[None], (ZLO,) + encoders.shape).reshape((ZLO * X,) + encoders.shape[1:])
    encoder_rows = lax.all_to_all(spread, ("zlo", "x"), 0, 0, tiled=True).reshape(-1, fw)
    encoder_own, encoder_other = over_feat(encoder_rows)

    window = lax.all_to_all(pieces, ("x", "core"), 0, 0, tiled=True).reshape(X, CORE, Y * height, tokens)
    partial = gram_of(place, window, target, swapped).reshape(X * Y, height, fw)
    partial = lax.all_to_all(partial, ("x", "y"), 0, 0, tiled=True).reshape(X, Y, height, fw)

    base = earlier[0] + earlier[1] + earlier[2]
    prefix = jnp.stack([(base + part).astype(jnp.bfloat16) for part in before])
    pieces = [lax.dynamic_index_in_dim(prefix, (x + k) % X, 0, keepdims=False) for k in range(X)]
    moved = [lax.ppermute(pieces[k], "x", ring(X, k)) for k in range(1, X)]
    prefix = jnp.stack([pieces[0]] + moved)

    virtual = virtual_of(place, prefix, encoder_own, encoder_other)
    virtual = [virtual[0]] + [lax.ppermute(virtual[k], "x", ring(X, X - k)) for k in range(1, X)]
    return weigh(place, partial, virtual)[None]


def solution(mesh):
    fine = Mesh(mesh.devices.reshape(ZLO, X, TGT, Y, CORE), ("zlo", "x", "tgt", "y", "core"))
    src = ("zlo", "x")
    in_specs = (
        P(src, None, FEAT),
        P(),
        P(src, "tgt", FEAT, None),
        P("tgt", src + FEAT, None),
    )
    out_specs = P(src, "tgt", FEAT, None)

    return jax.shard_map(per_device, mesh=fine, in_specs=in_specs, out_specs=out_specs, check_vma=False)
```

```python
import jax
import jax.numpy as jnp
from jax import lax
from jax.experimental import pallas as pl
from jax.experimental.pallas import tpu as pltpu
from jax.sharding import Mesh, PartitionSpec as P

ZLO, X, TGT, Y, CORE = 4, 4, 4, 4, 2
FEAT = ("y", "core")


def total_pairs(k):
    return [(z * TGT + b, z * TGT + b + k) for z in range(ZLO) for b in range(z, TGT - k)]


def window_pairs(k):
    return [(b * TGT + b, (b - k) * TGT + b) for b in range(k, TGT)]


def split_kernel(wide_ref, out_ref):
    tokens = out_ref.shape[2]
    for f in range(out_ref.shape[0]):
        out_ref[f] = wide_ref[:, f * tokens : (f + 1) * tokens]


def select_kernel(place_ref, ids_ref, sliced_ref, columns_ref, pieces_ref):
    feats, tokens = sliced_ref.shape
    width = ids_ref.shape[1]
    step = 128
    wide = jnp.broadcast_to(ids_ref[pl.ds(place_ref[4], 1), :], (step, width))
    columns = jnp.zeros((tokens, width), jnp.float32)
    for g in range(feats // step):
        part = sliced_ref[g * step : (g + 1) * step]
        chosen = (wide == g * step + lax.broadcasted_iota(jnp.int32, wide.shape, 0)).astype(jnp.bfloat16)
        columns += lax.dot_general(part, chosen, (((0,), (0,)), ((), ())), preferred_element_type=jnp.float32)
    columns_ref[...] = columns.astype(columns_ref.dtype)
    rows = columns.T.astype(pieces_ref.dtype)
    height = width // (Y * CORE)
    for y in range(Y):
        for c in range(CORE):
            f = y * CORE + c
            for x in range(X):
                pieces_ref[x * CORE + c, y * height : (y + 1) * height] = rows[f * height : (f + 1) * height]


def spread_kernel(rows_ref, out_ref):
    for z in range(ZLO):
        out_ref[z * X : (z + 1) * X] = rows_ref[...]


def prefix_kernel(place_ref, *refs):
    total_refs, decoders_ref, out_refs = refs[: TGT - 1], refs[TGT - 1], refs[TGT:]
    step = 16
    layers = decoders_ref.shape[0]

    def rows(i, carry):
        at = pl.ds(i * step, step)
        base = total_refs[0][at].astype(jnp.float32)
        for ref in total_refs[1:]:
            base += ref[at].astype(jnp.float32)
        written = [decoders_ref[k, at].astype(jnp.float32) for k in range(layers - 1)]
        for r in range(X):
            layer = (place_ref[0] + r) % X
            out = base
            for k in range(layers - 1):
                counts = jnp.logical_and(k < layer, k >= place_ref[5])
                out += written[k] * jnp.where(counts, 1.0, 0.0)
            out_refs[r][at] = out.astype(jnp.bfloat16)
        return carry

    lax.fori_loop(0, decoders_ref.shape[1] // step, rows, 0)


def virtual_kernel(place_ref, *refs):
    prefix_refs, own_refs, other_ref, out_refs, rows_ref = refs[:X], refs[X : X + Y], refs[X + Y], refs[X + Y + 1 : -1], refs[-1]
    groups, slices, depth, width = rows_ref.shape
    core = place_ref[2]
    for r in range(Y):
        row = (place_ref[1] + Y - r) % Y
        rows_ref[:, row * CORE + core] = own_refs[r][...].reshape(groups, depth, width)
        rows_ref[:, row * CORE + 1 - core] = other_ref[r].reshape(groups, depth, width)
    height = prefix_refs[0].shape[0]
    chunk = slices * depth
    total = jnp.zeros((X * height, width), jnp.float32)
    for g in range(groups):
        left = jnp.concatenate([ref[:, g * chunk : (g + 1) * chunk] for ref in prefix_refs], 0)
        total += jnp.dot(left, rows_ref[g].reshape(chunk, width), preferred_element_type=jnp.float32)
    for r in range(X):
        out_refs[r][...] = total[r * height : (r + 1) * height]


def gram_kernel(place_ref, window_ref, own_ref, other_ref, out_ref):
    core = place_ref[2]
    for q in range(window_ref.shape[0]):
        part = jnp.dot(window_ref[q, core], own_ref[...], preferred_element_type=jnp.float32)
        part += jnp.dot(window_ref[q, 1 - core], other_ref[...], preferred_element_type=jnp.float32)
        out_ref[q] = part.astype(out_ref.dtype)


def weigh_kernel(place_ref, gram_ref, *refs):
    virtual_refs, out_ref = refs[:-1], refs[-1]
    token_count = place_ref[3].astype(jnp.float32)
    for r in range(X):
        layer = (place_ref[0] + r) % X
        gram = gram_ref[layer, 0].astype(jnp.float32)
        for row in range(1, Y):
            gram += gram_ref[layer, row].astype(jnp.float32)
        out_ref[layer] = virtual_refs[r][...] * (gram / token_count)


SMEM = pl.BlockSpec(memory_space=pltpu.SMEM)
VMEM = pl.BlockSpec(memory_space=pltpu.VMEM)


def split(wide, slices):
    feats, token_count = wide.shape
    return pl.pallas_call(
        split_kernel,
        out_shape=jax.ShapeDtypeStruct((slices, feats, token_count // slices), wide.dtype),
        in_specs=[VMEM],
        out_specs=VMEM,
    )(wide)


def select(place, window_ids, sliced):
    tokens, width = sliced.shape[1], window_ids.shape[1]
    return pl.pallas_call(
        select_kernel,
        out_shape=(
            jax.ShapeDtypeStruct((tokens, width), jnp.bfloat16),
            jax.ShapeDtypeStruct((X * CORE, width // CORE, tokens), jnp.bfloat16),
        ),
        in_specs=[SMEM, VMEM, VMEM],
        out_specs=(VMEM, VMEM),
    )(place, window_ids, sliced)


def spread_of(rows):
    return pl.pallas_call(
        spread_kernel,
        out_shape=jax.ShapeDtypeStruct((ZLO * rows.shape[0],) + rows.shape[1:], rows.dtype),
        in_specs=[VMEM],
        out_specs=VMEM,
    )(rows)


def prefix_of(place, totals, decoders):
    piece = jax.ShapeDtypeStruct(decoders.shape[1:], jnp.bfloat16)
    return pl.pallas_call(
        prefix_kernel,
        out_shape=[piece] * X,
        in_specs=[SMEM] + [VMEM] * (len(totals) + 1),
        out_specs=[VMEM] * X,
    )(place, *totals, decoders)


def virtual_of(place, prefix, own, other):
    height, depth = prefix[0].shape
    width = other.shape[2]
    groups = ZLO * X
    return pl.pallas_call(
        virtual_kernel,
        out_shape=[jax.ShapeDtypeStruct((height, width), jnp.float32)] * X,
        in_specs=[SMEM] + [VMEM] * (len(prefix) + len(own) + 1),
        out_specs=[VMEM] * X,
        scratch_shapes=[pltpu.VMEM((groups, Y * CORE, depth // (groups * Y * CORE), width), jnp.bfloat16)],
    )(place, *prefix, *own, other)


def gram_of(place, window, own, other):
    return pl.pallas_call(
        gram_kernel,
        out_shape=jax.ShapeDtypeStruct((X, window.shape[2], own.shape[1]), jnp.bfloat16),
        in_specs=[SMEM, VMEM, VMEM, VMEM],
        out_specs=VMEM,
    )(place, window, own, other)


def weigh(place, gram, virtual):
    return pl.pallas_call(
        weigh_kernel,
        out_shape=jax.ShapeDtypeStruct((X,) + virtual[0].shape, jnp.float32),
        in_specs=[SMEM, VMEM] + [VMEM] * len(virtual),
        out_specs=VMEM,
    )(place, gram, *virtual)


def ring(n, k):
    return [(i, (i + k) % n) for i in range(n)]


def over_feat(piece):
    others = [lax.ppermute(piece, "y", ring(Y, k)) for k in range(1, Y)]
    own = [piece] + others
    return own, lax.ppermute(jnp.stack(own), "core", ring(CORE, 1))


def per_device(activations, window_ids, decoders, encoders):
    zlo = lax.axis_index("zlo")
    block = lax.axis_index("tgt")
    x = lax.axis_index("x")
    source = zlo * X + x
    token_count, local_feats = activations.shape[1:]
    targets, height = decoders.shape[1:3]
    fw = window_ids.shape[1]
    slices = Y * CORE
    tokens = token_count // slices

    place = [x, lax.axis_index("y"), lax.axis_index("core"), token_count, source, source - block * targets]
    place = jnp.stack(place).astype(jnp.int32)

    live = (block * targets + jnp.arange(targets) >= source).astype(jnp.float32)
    total = jnp.sum(decoders[0].astype(jnp.float32) * live[:, None, None], 0).astype(jnp.bfloat16)
    earlier = [lax.ppermute(total, ("zlo", "tgt"), total_pairs(k)) for k in (3, 2, 1)]

    by_tokens = split(activations[0].T, slices)
    sliced = lax.all_to_all(by_tokens, FEAT, 0, 0, tiled=True).reshape(slices * local_feats, tokens)
    columns, pieces = select(place, window_ids, sliced)

    parts = [lax.ppermute(columns, ("zlo", "tgt"), window_pairs(k)) for k in (3, 2, 1)]
    target = jnp.where(zlo == block, columns, parts[0] + parts[1] + parts[2])
    swapped = lax.ppermute(target, "core", ring(CORE, 1))

    spread = spread_of(encoders)
    encoder_rows = lax.all_to_all(spread, ("zlo", "x"), 0, 0, tiled=True).reshape(-1, fw)
    encoder_own, encoder_other = over_feat(encoder_rows)

    window = lax.all_to_all(pieces, ("x", "core"), 0, 0, tiled=True).reshape(X, CORE, Y * height, tokens)
    partial = gram_of(place, window, target, swapped).reshape(X * Y, height, fw)
    partial = lax.all_to_all(partial, ("x", "y"), 0, 0, tiled=True).reshape(X, Y, height, fw)

    pieces = prefix_of(place, earlier, decoders[0])
    moved = [lax.ppermute(pieces[k], "x", ring(X, k)) for k in range(1, X)]
    virtual = virtual_of(place, [pieces[0]] + moved, encoder_own, encoder_other)
    virtual = [virtual[0]] + [lax.ppermute(virtual[k], "x", ring(X, X - k)) for k in range(1, X)]
    return weigh(place, partial, virtual)[None]


def solution(mesh):
    fine = Mesh(mesh.devices.reshape(ZLO, X, TGT, Y, CORE), ("zlo", "x", "tgt", "y", "core"))
    src = ("zlo", "x")
    in_specs = (
        P(src, None, FEAT),
        P(),
        P(src, "tgt", FEAT, None),
        P("tgt", src + FEAT, None),
    )
    out_specs = P(src, "tgt", FEAT, None)

    return jax.shard_map(per_device, mesh=fine, in_specs=in_specs, out_specs=out_specs, check_vma=False)
```

```python
import functools

import jax
import jax.numpy as jnp
from jax import lax
from jax.experimental import pallas as pl
from jax.experimental.pallas import tpu as pltpu
from jax.sharding import Mesh, PartitionSpec as P

ZLO, X, TGT, Y, CORE = 4, 4, 4, 4, 2
FEAT = ("y", "core")


def total_pairs(k):
    return [(z * TGT + b, z * TGT + b + k) for z in range(ZLO) for b in range(z, TGT - k)]


def window_pairs(k):
    return [(b * TGT + b, (b - k) * TGT + b) for b in range(k, TGT)]


def split_kernel(wide_ref, out_ref):
    tokens = out_ref.shape[2]
    for f in range(out_ref.shape[0]):
        out_ref[f] = wide_ref[:, f * tokens : (f + 1) * tokens]


def select_kernel(place_ref, ids_ref, sliced_ref, columns_ref, pieces_ref):
    feats, tokens = sliced_ref.shape
    width = ids_ref.shape[1]
    step = 128
    wide = jnp.broadcast_to(ids_ref[pl.ds(place_ref[3], 1), :], (step, width))
    columns = jnp.zeros((tokens, width), jnp.float32)
    for g in range(feats // step):
        part = sliced_ref[g * step : (g + 1) * step]
        chosen = (wide == g * step + lax.broadcasted_iota(jnp.int32, wide.shape, 0)).astype(jnp.bfloat16)
        columns += lax.dot_general(part, chosen, (((0,), (0,)), ((), ())), preferred_element_type=jnp.float32)
    columns_ref[...] = columns.astype(columns_ref.dtype)
    rows = columns.T.astype(pieces_ref.dtype)
    height = width // (Y * CORE)
    for y in range(Y):
        for c in range(CORE):
            f = y * CORE + c
            for x in range(X):
                pieces_ref[x * CORE + c, y * height : (y + 1) * height] = rows[f * height : (f + 1) * height]


def spread_kernel(rows_ref, out_ref):
    for z in range(ZLO):
        out_ref[z * X : (z + 1) * X] = rows_ref[...]


def prefix_kernel(place_ref, *refs):
    total_refs, decoders_ref, out_refs = refs[: TGT - 1], refs[TGT - 1], refs[TGT:]
    step = 16
    layers = decoders_ref.shape[0]

    def rows(i, carry):
        at = pl.ds(i * step, step)
        base = total_refs[0][at].astype(jnp.float32)
        for ref in total_refs[1:]:
            base += ref[at].astype(jnp.float32)
        written = [decoders_ref[k, at].astype(jnp.float32) for k in range(layers - 1)]
        for r in range(X):
            layer = (place_ref[0] + r) % X
            out = base
            for k in range(layers - 1):
                counts = jnp.logical_and(k < layer, k >= place_ref[4])
                out += written[k] * jnp.where(counts, 1.0, 0.0)
            out_refs[r][at] = out.astype(jnp.bfloat16)
        return carry

    lax.fori_loop(0, decoders_ref.shape[1] // step, rows, 0)


def virtual_kernel(place_ref, *refs):
    prefix_refs, own_refs, other_ref, out_refs, rows_ref = refs[:X], refs[X : X + Y], refs[X + Y], refs[X + Y + 1 : -1], refs[-1]
    groups, slices, depth, width = rows_ref.shape
    core = place_ref[2]
    for r in range(Y):
        row = (place_ref[1] + Y - r) % Y
        rows_ref[:, row * CORE + core] = own_refs[r][...].reshape(groups, depth, width)
        rows_ref[:, row * CORE + 1 - core] = other_ref[r].reshape(groups, depth, width)
    height = prefix_refs[0].shape[0]
    chunk = slices * depth
    total = jnp.zeros((X * height, width), jnp.float32)
    for g in range(0, groups, 2):
        left = jnp.concatenate([ref[:, g * chunk : (g + 2) * chunk] for ref in prefix_refs], 0)
        right = rows_ref[g : g + 2].reshape(2 * chunk, width)
        total += jnp.dot(left, right, preferred_element_type=jnp.float32)
    for r in range(X):
        out_refs[r][...] = total[r * height : (r + 1) * height]


def gram_kernel(place_ref, window_ref, own_ref, other_ref, out_ref):
    core = place_ref[2]
    for q in range(window_ref.shape[0]):
        part = jnp.dot(window_ref[q, core], own_ref[...], preferred_element_type=jnp.float32)
        part += jnp.dot(window_ref[q, 1 - core], other_ref[...], preferred_element_type=jnp.float32)
        out_ref[q] = part.astype(out_ref.dtype)


def weigh_kernel(scale, place_ref, gram_ref, *refs):
    virtual_refs, out_ref = refs[:-1], refs[-1]
    for r in range(X):
        layer = (place_ref[0] + r) % X
        gram = gram_ref[layer, 0].astype(jnp.float32)
        for row in range(1, Y):
            gram += gram_ref[layer, row].astype(jnp.float32)
        out_ref[layer] = virtual_refs[r][...] * (gram * scale)


SMEM = pl.BlockSpec(memory_space=pltpu.SMEM)
VMEM = pl.BlockSpec(memory_space=pltpu.VMEM)


def split(wide, slices):
    feats, token_count = wide.shape
    return pl.pallas_call(
        split_kernel,
        out_shape=jax.ShapeDtypeStruct((slices, feats, token_count // slices), wide.dtype),
        in_specs=[VMEM],
        out_specs=VMEM,
    )(wide)


def select(place, window_ids, sliced):
    tokens, width = sliced.shape[1], window_ids.shape[1]
    return pl.pallas_call(
        select_kernel,
        out_shape=(
            jax.ShapeDtypeStruct((tokens, width), jnp.bfloat16),
            jax.ShapeDtypeStruct((X * CORE, width // CORE, tokens), jnp.bfloat16),
        ),
        in_specs=[SMEM, VMEM, VMEM],
        out_specs=(VMEM, VMEM),
    )(place, window_ids, sliced)


def spread_of(rows):
    return pl.pallas_call(
        spread_kernel,
        out_shape=jax.ShapeDtypeStruct((ZLO * rows.shape[0],) + rows.shape[1:], rows.dtype),
        in_specs=[VMEM],
        out_specs=VMEM,
    )(rows)


def prefix_of(place, totals, decoders):
    piece = jax.ShapeDtypeStruct(decoders.shape[1:], jnp.bfloat16)
    return pl.pallas_call(
        prefix_kernel,
        out_shape=[piece] * X,
        in_specs=[SMEM] + [VMEM] * (len(totals) + 1),
        out_specs=[VMEM] * X,
    )(place, *totals, decoders)


def virtual_of(place, prefix, own, other):
    height, depth = prefix[0].shape
    width = other.shape[2]
    groups = ZLO * X
    return pl.pallas_call(
        virtual_kernel,
        out_shape=[jax.ShapeDtypeStruct((height, width), jnp.float32)] * X,
        in_specs=[SMEM] + [VMEM] * (len(prefix) + len(own) + 1),
        out_specs=[VMEM] * X,
        scratch_shapes=[pltpu.VMEM((groups, Y * CORE, depth // (groups * Y * CORE), width), jnp.bfloat16)],
    )(place, *prefix, *own, other)


def gram_of(place, window, own, other):
    return pl.pallas_call(
        gram_kernel,
        out_shape=jax.ShapeDtypeStruct((X, window.shape[2], own.shape[1]), jnp.bfloat16),
        in_specs=[SMEM, VMEM, VMEM, VMEM],
        out_specs=VMEM,
    )(place, window, own, other)


def weigh(place, gram, virtual, token_count):
    return pl.pallas_call(
        functools.partial(weigh_kernel, 1.0 / token_count),
        out_shape=jax.ShapeDtypeStruct((X,) + virtual[0].shape, jnp.float32),
        in_specs=[SMEM, VMEM] + [VMEM] * len(virtual),
        out_specs=VMEM,
    )(place, gram, *virtual)


def ring(n, k):
    return [(i, (i + k) % n) for i in range(n)]


def over_feat(piece):
    others = [lax.ppermute(piece, "y", ring(Y, k)) for k in range(1, Y)]
    own = [piece] + others
    return own, lax.ppermute(jnp.stack(own), "core", ring(CORE, 1))


def per_device(activations, window_ids, decoders, encoders):
    zlo = lax.axis_index("zlo")
    block = lax.axis_index("tgt")
    x = lax.axis_index("x")
    source = zlo * X + x
    token_count, local_feats = activations.shape[1:]
    targets, height = decoders.shape[1:3]
    fw = window_ids.shape[1]
    slices = Y * CORE
    tokens = token_count // slices

    place = [x, lax.axis_index("y"), lax.axis_index("core"), source, source - block * targets]
    place = jnp.stack(place).astype(jnp.int32)

    spread = spread_of(encoders)
    encoder_rows = lax.all_to_all(spread, ("zlo", "x"), 0, 0, tiled=True).reshape(-1, fw)
    encoder_own, encoder_other = over_feat(encoder_rows)

    live = (block * targets + jnp.arange(targets) >= source).astype(jnp.float32)
    total = jnp.sum(decoders[0].astype(jnp.float32) * live[:, None, None], 0).astype(jnp.bfloat16)
    earlier = [lax.ppermute(total, ("zlo", "tgt"), total_pairs(k)) for k in (3, 2, 1)]

    by_tokens = split(activations[0].T, slices)
    sliced = lax.all_to_all(by_tokens, FEAT, 0, 0, tiled=True).reshape(slices * local_feats, tokens)
    columns, pieces = select(place, window_ids, sliced)

    parts = [lax.ppermute(columns, ("zlo", "tgt"), window_pairs(k)) for k in (3, 2, 1)]
    target = jnp.where(zlo == block, columns, parts[0] + parts[1] + parts[2])
    swapped = lax.ppermute(target, "core", ring(CORE, 1))

    window = lax.all_to_all(pieces, ("x", "core"), 0, 0, tiled=True).reshape(X, CORE, Y * height, tokens)
    partial = gram_of(place, window, target, swapped).reshape(X * Y, height, fw)
    partial = lax.all_to_all(partial, ("x", "y"), 0, 0, tiled=True).reshape(X, Y, height, fw)

    pieces = prefix_of(place, earlier, decoders[0])
    moved = [lax.ppermute(pieces[k], "x", ring(X, k)) for k in range(1, X)]
    virtual = virtual_of(place, [pieces[0]] + moved, encoder_own, encoder_other)
    virtual = [virtual[0]] + [lax.ppermute(virtual[k], "x", ring(X, X - k)) for k in range(1, X)]
    return weigh(place, partial, virtual, token_count)[None]


def solution(mesh):
    fine = Mesh(mesh.devices.reshape(ZLO, X, TGT, Y, CORE), ("zlo", "x", "tgt", "y", "core"))
    src = ("zlo", "x")
    in_specs = (
        P(src, None, FEAT),
        P(),
        P(src, "tgt", FEAT, None),
        P("tgt", src + FEAT, None),
    )
    out_specs = P(src, "tgt", FEAT, None)

    return jax.shard_map(per_device, mesh=fine, in_specs=in_specs, out_specs=out_specs, check_vma=False)
```

```python
import functools

import jax
import jax.numpy as jnp
from jax import lax
from jax.experimental import pallas as pl
from jax.experimental.pallas import tpu as pltpu
from jax.sharding import Mesh, PartitionSpec as P

ZLO, X, TGT, Y, CORE = 4, 4, 4, 4, 2
FEAT = ("y", "core")


def total_pairs(k):
    return [(z * TGT + b, z * TGT + b + k) for z in range(ZLO) for b in range(z, TGT - k)]


def window_pairs(k):
    return [(b * TGT + b, (b - k) * TGT + b) for b in range(k, TGT)]


def split_kernel(wide_ref, out_ref):
    tokens = out_ref.shape[2]
    for f in range(out_ref.shape[0]):
        out_ref[f] = wide_ref[:, f * tokens : (f + 1) * tokens]


def select_kernel(place_ref, ids_ref, sliced_ref, columns_ref, pieces_ref):
    feats, tokens = sliced_ref.shape
    width = ids_ref.shape[1]
    step = 128
    wide = jnp.broadcast_to(ids_ref[pl.ds(place_ref[3], 1), :], (step, width))
    columns = jnp.zeros((tokens, width), jnp.float32)
    for g in range(feats // step):
        part = sliced_ref[g * step : (g + 1) * step]
        chosen = (wide == g * step + lax.broadcasted_iota(jnp.int32, wide.shape, 0)).astype(jnp.bfloat16)
        columns += lax.dot_general(part, chosen, (((0,), (0,)), ((), ())), preferred_element_type=jnp.float32)
    columns_ref[...] = columns.astype(columns_ref.dtype)
    rows = columns.T.astype(pieces_ref.dtype)
    height = width // (Y * CORE)
    for y in range(Y):
        for c in range(CORE):
            f = y * CORE + c
            for x in range(X):
                pieces_ref[x * CORE + c, y * height : (y + 1) * height] = rows[f * height : (f + 1) * height]


def prefix_kernel(place_ref, *refs):
    total_refs, decoders_ref, out_ref = refs[:-2], refs[-2], refs[-1]
    step = 16
    layers = decoders_ref.shape[0]

    def rows(i, carry):
        at = pl.ds(i * step, step)
        base = total_refs[0][at].astype(jnp.float32)
        for ref in total_refs[1:]:
            base += ref[at].astype(jnp.float32)
        written = [decoders_ref[k, at].astype(jnp.float32) for k in range(layers - 1)]
        out_ref[0, at] = base.astype(jnp.bfloat16)
        for k in range(layers - 1):
            base += written[k] * jnp.where(k >= place_ref[4], 1.0, 0.0)
            out_ref[k + 1, at] = base.astype(jnp.bfloat16)
        return carry

    lax.fori_loop(0, decoders_ref.shape[1] // step, rows, 0)


def virtual_kernel(place_ref, prefix_ref, near_ref, far_ref, other_ref, *refs):
    out_refs, rows_ref = refs[:-1], refs[-1]
    groups, slices, depth, width = rows_ref.shape
    x, y, core = place_ref[0], place_ref[1], place_ref[2]
    for r in range(Y):
        row = jnp.bitwise_xor(y, r)
        own = near_ref[r] if r < Y // 2 else far_ref[r - Y // 2]
        rows_ref[:, row * CORE + core] = own.reshape(groups, depth, width)
        rows_ref[:, row * CORE + 1 - core] = other_ref[r].reshape(groups, depth, width)
    height = prefix_ref.shape[1]
    chunk = slices * depth
    order = [(x + X - r) % X for r in range(X)]
    total = jnp.zeros((X * height, width), jnp.float32)
    for g in range(0, groups, 2):
        left = jnp.concatenate([prefix_ref[q, :, g * chunk : (g + 2) * chunk] for q in order], 0)
        right = rows_ref[g : g + 2].reshape(2 * chunk, width)
        total += jnp.dot(left, right, preferred_element_type=jnp.float32)
    for r in range(X):
        out_refs[r][...] = total[r * height : (r + 1) * height]


def gram_kernel(place_ref, window_ref, own_ref, other_ref, out_ref):
    core = place_ref[2]
    for q in range(window_ref.shape[0]):
        part = jnp.dot(window_ref[q, core], own_ref[...], preferred_element_type=jnp.float32)
        part += jnp.dot(window_ref[q, 1 - core], other_ref[...], preferred_element_type=jnp.float32)
        out_ref[q] = part.astype(out_ref.dtype)


def weigh_kernel(scale, place_ref, gram_ref, *refs):
    virtual_refs, out_ref = refs[:-1], refs[-1]
    for r in range(X):
        layer = (place_ref[0] + r) % X
        gram = gram_ref[layer, 0].astype(jnp.float32)
        for row in range(1, Y):
            gram += gram_ref[layer, row].astype(jnp.float32)
        out_ref[layer] = virtual_refs[r][...] * (gram * scale)


SMEM = pl.BlockSpec(memory_space=pltpu.SMEM)
VMEM = pl.BlockSpec(memory_space=pltpu.VMEM)


def split(wide, slices):
    feats, token_count = wide.shape
    return pl.pallas_call(
        split_kernel,
        out_shape=jax.ShapeDtypeStruct((slices, feats, token_count // slices), wide.dtype),
        in_specs=[VMEM],
        out_specs=VMEM,
    )(wide)


def select(place, window_ids, sliced):
    tokens, width = sliced.shape[1], window_ids.shape[1]
    return pl.pallas_call(
        select_kernel,
        out_shape=(
            jax.ShapeDtypeStruct((tokens, width), jnp.bfloat16),
            jax.ShapeDtypeStruct((X * CORE, width // CORE, tokens), jnp.bfloat16),
        ),
        in_specs=[SMEM, VMEM, VMEM],
        out_specs=(VMEM, VMEM),
    )(place, window_ids, sliced)


def prefix_of(place, totals, decoders):
    return pl.pallas_call(
        prefix_kernel,
        out_shape=jax.ShapeDtypeStruct(decoders.shape, jnp.bfloat16),
        in_specs=[SMEM] + [VMEM] * (len(totals) + 1),
        out_specs=VMEM,
    )(place, *totals, decoders)


def virtual_of(place, prefix, near, far, other):
    height, depth = prefix.shape[1:]
    width = other.shape[2]
    groups = ZLO * X
    return pl.pallas_call(
        virtual_kernel,
        out_shape=[jax.ShapeDtypeStruct((height, width), jnp.float32)] * X,
        in_specs=[SMEM] + [VMEM] * 4,
        out_specs=[VMEM] * X,
        scratch_shapes=[pltpu.VMEM((groups, Y * CORE, depth // (groups * Y * CORE), width), jnp.bfloat16)],
    )(place, prefix, near, far, other)


def gram_of(place, window, own, other):
    return pl.pallas_call(
        gram_kernel,
        out_shape=jax.ShapeDtypeStruct((X, window.shape[2], own.shape[1]), jnp.bfloat16),
        in_specs=[SMEM, VMEM, VMEM, VMEM],
        out_specs=VMEM,
    )(place, window, own, other)


def weigh(place, gram, virtual, token_count):
    return pl.pallas_call(
        functools.partial(weigh_kernel, 1.0 / token_count),
        out_shape=jax.ShapeDtypeStruct((X,) + virtual[0].shape, jnp.float32),
        in_specs=[SMEM, VMEM] + [VMEM] * len(virtual),
        out_specs=VMEM,
    )(place, gram, *virtual)


def ring(n, k):
    return [(i, (i + k) % n) for i in range(n)]


def over_feat(piece):
    near = jnp.stack([piece, lax.ppermute(piece, "y", [(i, i ^ 1) for i in range(Y)])])
    far = lax.ppermute(near, "y", [(i, i ^ 2) for i in range(Y)])
    other = lax.ppermute(jnp.concatenate([near, far]), "core", ring(CORE, 1))
    return near, far, other


def per_device(activations, window_ids, decoders, encoders):
    zlo = lax.axis_index("zlo")
    block = lax.axis_index("tgt")
    x = lax.axis_index("x")
    source = zlo * X + x
    token_count, local_feats = activations.shape[1:]
    targets, height = decoders.shape[1:3]
    fw = window_ids.shape[1]
    slices = Y * CORE
    tokens = token_count // slices

    place = [x, lax.axis_index("y"), lax.axis_index("core"), source, source - block * targets]
    place = jnp.stack(place).astype(jnp.int32)

    spread = jnp.broadcast_to(encoders[None], (ZLO,) + encoders.shape).reshape((ZLO * X,) + encoders.shape[1:])
    encoder_rows = lax.all_to_all(spread, ("zlo", "x"), 0, 0, tiled=True).reshape(-1, fw)
    encoder = over_feat(encoder_rows)

    live = (block * targets + jnp.arange(targets) >= source).astype(jnp.float32)
    total = jnp.sum(decoders[0].astype(jnp.float32) * live[:, None, None], 0).astype(jnp.bfloat16)
    earlier = [lax.ppermute(total, ("zlo", "tgt"), total_pairs(k)) for k in (3, 2, 1)]

    by_tokens = split(activations[0].T, slices)
    sliced = lax.all_to_all(by_tokens, FEAT, 0, 0, tiled=True).reshape(slices * local_feats, tokens)
    columns, pieces = select(place, window_ids, sliced)

    parts = [lax.ppermute(columns, ("zlo", "tgt"), window_pairs(k)) for k in (3, 2, 1)]
    target = jnp.where(zlo == block, columns, parts[0] + parts[1] + parts[2])
    swapped = lax.ppermute(target, "core", ring(CORE, 1))

    window = lax.all_to_all(pieces, ("x", "core"), 0, 0, tiled=True).reshape(X, CORE, Y * height, tokens)
    partial = gram_of(place, window, target, swapped).reshape(X * Y, height, fw)
    partial = lax.all_to_all(partial, ("x", "y"), 0, 0, tiled=True).reshape(X, Y, height, fw)

    prefix = prefix_of(place, earlier, decoders[0])
    prefix = lax.all_to_all(prefix, "x", 0, 0, tiled=True)
    virtual = virtual_of(place, prefix, *encoder)
    virtual = [virtual[0]] + [lax.ppermute(virtual[k], "x", ring(X, X - k)) for k in range(1, X)]
    return weigh(place, partial, virtual, token_count)[None]


def solution(mesh):
    fine = Mesh(mesh.devices.reshape(ZLO, X, TGT, Y, CORE), ("zlo", "x", "tgt", "y", "core"))
    src = ("zlo", "x")
    in_specs = (
        P(src, None, FEAT),
        P(),
        P(src, "tgt", FEAT, None),
        P("tgt", src + FEAT, None),
    )
    out_specs = P(src, "tgt", FEAT, None)

    return jax.shard_map(per_device, mesh=fine, in_specs=in_specs, out_specs=out_specs, check_vma=False)
```

```python
import functools

import jax
import jax.numpy as jnp
from jax import lax
from jax.experimental import pallas as pl
from jax.experimental.pallas import tpu as pltpu
from jax.sharding import Mesh, PartitionSpec as P

ZLO, X, TGT, Y, CORE = 4, 4, 4, 4, 2
FEAT = ("y", "core")


def total_pairs(k):
    return [(z * TGT + b, z * TGT + b + k) for z in range(ZLO) for b in range(z, TGT - k)]


def window_pairs(k):
    return [(b * TGT + b, (b - k) * TGT + b) for b in range(k, TGT)]


def split_kernel(wide_ref, out_ref):
    tokens = out_ref.shape[2]
    for f in range(out_ref.shape[0]):
        out_ref[f] = wide_ref[:, f * tokens : (f + 1) * tokens]


def select_kernel(ids_ref, sliced_ref, columns_ref, pieces_ref):
    feats, tokens = sliced_ref.shape
    width = ids_ref.shape[1]
    step = 128
    wide = jnp.broadcast_to(ids_ref[pl.ds(lax.axis_index("zlo") * X + lax.axis_index("x"), 1), :], (step, width))
    columns = jnp.zeros((tokens, width), jnp.float32)
    for g in range(feats // step):
        part = sliced_ref[g * step : (g + 1) * step]
        chosen = (wide == g * step + lax.broadcasted_iota(jnp.int32, wide.shape, 0)).astype(jnp.bfloat16)
        columns += lax.dot_general(part, chosen, (((0,), (0,)), ((), ())), preferred_element_type=jnp.float32)
    columns_ref[...] = columns.astype(columns_ref.dtype)
    rows = columns.T.astype(pieces_ref.dtype)
    height = width // (Y * CORE)
    for y in range(Y):
        for c in range(CORE):
            f = y * CORE + c
            for x in range(X):
                pieces_ref[x * CORE + c, y * height : (y + 1) * height] = rows[f * height : (f + 1) * height]


def prefix_kernel(*refs):
    total_refs, decoders_ref, out_refs = refs[: TGT - 1], refs[TGT - 1], refs[TGT:]
    layers = decoders_ref.shape[0]
    x = lax.axis_index("x")
    first = lax.axis_index("zlo") * X + x - lax.axis_index("tgt") * layers
    base = total_refs[0][...].astype(jnp.float32)
    for ref in total_refs[1:]:
        base += ref[...].astype(jnp.float32)
    written = [decoders_ref[k].astype(jnp.float32) for k in range(layers - 1)]
    for r in range(X):
        layer = (x + r) % X
        out = base
        for k in range(layers - 1):
            counts = jnp.logical_and(k < layer, k >= first)
            out += written[k] * jnp.where(counts, 1.0, 0.0)
        out_refs[r][...] = out.astype(jnp.bfloat16)


def virtual_kernel(*refs):
    prefix_refs, own_refs, other_ref, out_refs, rows_ref = refs[:X], refs[X : X + Y], refs[X + Y], refs[X + Y + 1 : -1], refs[-1]
    groups, slices, depth, width = rows_ref.shape
    y, core = lax.axis_index("y"), lax.axis_index("core")
    for r in range(Y):
        row = (y + Y - r) % Y
        rows_ref[:, row * CORE + core] = own_refs[r][...].reshape(groups, depth, width)
        rows_ref[:, row * CORE + 1 - core] = other_ref[r].reshape(groups, depth, width)
    height = prefix_refs[0].shape[0]
    chunk = slices * depth
    total = jnp.zeros((X * height, width), jnp.float32)
    for g in range(0, groups, 2):
        left = jnp.concatenate([ref[:, g * chunk : (g + 2) * chunk] for ref in prefix_refs], 0)
        right = rows_ref[g : g + 2].reshape(2 * chunk, width)
        total += jnp.dot(left, right, preferred_element_type=jnp.float32)
    for r in range(X):
        out_refs[r][...] = total[r * height : (r + 1) * height]


def gram_kernel(window_ref, own_ref, other_ref, out_ref):
    core = lax.axis_index("core")
    part = jnp.dot(window_ref[0, core], own_ref[...], preferred_element_type=jnp.float32)
    part += jnp.dot(window_ref[0, 1 - core], other_ref[...], preferred_element_type=jnp.float32)
    out_ref[0] = part.astype(out_ref.dtype)


def weigh_kernel(scale, gram_ref, *refs):
    virtual_refs, out_ref = refs[:-1], refs[-1]
    gram = gram_ref[0, 0].astype(jnp.float32)
    for row in range(1, Y):
        gram += gram_ref[0, row].astype(jnp.float32)
    gram = gram * scale
    piece = (pl.program_id(0) + X - lax.axis_index("x")) % X
    for r in range(X):

        @pl.when(piece == r)
        def _(r=r):
            out_ref[0] = virtual_refs[r][...] * gram


VMEM = pl.BlockSpec(memory_space=pltpu.VMEM)


def split(wide, slices):
    feats, token_count = wide.shape
    return pl.pallas_call(
        split_kernel,
        out_shape=jax.ShapeDtypeStruct((slices, feats, token_count // slices), wide.dtype),
        in_specs=[VMEM],
        out_specs=VMEM,
    )(wide)


def select(window_ids, sliced):
    tokens, width = sliced.shape[1], window_ids.shape[1]
    return pl.pallas_call(
        select_kernel,
        out_shape=(
            jax.ShapeDtypeStruct((tokens, width), jnp.bfloat16),
            jax.ShapeDtypeStruct((X * CORE, width // CORE, tokens), jnp.bfloat16),
        ),
        in_specs=[VMEM, VMEM],
        out_specs=(VMEM, VMEM),
    )(window_ids, sliced)


def prefix_of(totals, decoders):
    layers, height, depth = decoders.shape
    step = 16
    rows = pl.BlockSpec((step, depth), lambda i: (i, 0))
    return pl.pallas_call(
        prefix_kernel,
        grid=(height // step,),
        out_shape=[jax.ShapeDtypeStruct((height, depth), jnp.bfloat16)] * X,
        in_specs=[rows] * len(totals) + [pl.BlockSpec((layers, step, depth), lambda i: (0, i, 0))],
        out_specs=[rows] * X,
    )(*totals, decoders)


def virtual_of(prefix, own, other):
    height, depth = prefix[0].shape
    width = other.shape[2]
    groups = ZLO * X
    return pl.pallas_call(
        virtual_kernel,
        out_shape=[jax.ShapeDtypeStruct((height, width), jnp.float32)] * X,
        in_specs=[VMEM] * (len(prefix) + len(own) + 1),
        out_specs=[VMEM] * X,
        scratch_shapes=[pltpu.VMEM((groups, Y * CORE, depth // (groups * Y * CORE), width), jnp.bfloat16)],
    )(*prefix, *own, other)


def gram_of(window, own, other):
    sources, halves, height, tokens = window.shape
    width = own.shape[1]
    return pl.pallas_call(
        gram_kernel,
        grid=(sources,),
        out_shape=jax.ShapeDtypeStruct((sources, height, width), jnp.bfloat16),
        in_specs=[pl.BlockSpec((1, halves, height, tokens), lambda q: (q, 0, 0, 0)), VMEM, VMEM],
        out_specs=pl.BlockSpec((1, height, width), lambda q: (q, 0, 0)),
    )(window, own, other)


def weigh(gram, virtual, token_count):
    layers, rows, height, width = gram.shape
    return pl.pallas_call(
        functools.partial(weigh_kernel, 1.0 / token_count),
        grid=(layers,),
        out_shape=jax.ShapeDtypeStruct((layers, height, width), jnp.float32),
        in_specs=[pl.BlockSpec((1, rows, height, width), lambda k: (k, 0, 0, 0))] + [VMEM] * len(virtual),
        out_specs=pl.BlockSpec((1, height, width), lambda k: (k, 0, 0)),
    )(gram, *virtual)


def ring(n, k):
    return [(i, (i + k) % n) for i in range(n)]


def over_feat(piece):
    others = [lax.ppermute(piece, "y", ring(Y, k)) for k in range(1, Y)]
    own = [piece] + others
    return own, lax.ppermute(jnp.stack(own), "core", ring(CORE, 1))


def per_device(activations, window_ids, decoders, encoders):
    zlo = lax.axis_index("zlo")
    block = lax.axis_index("tgt")
    x = lax.axis_index("x")
    source = zlo * X + x
    token_count, local_feats = activations.shape[1:]
    targets, height = decoders.shape[1:3]
    fw = window_ids.shape[1]
    slices = Y * CORE
    tokens = token_count // slices

    spread = jnp.broadcast_to(encoders[None], (ZLO,) + encoders.shape).reshape((ZLO * X,) + encoders.shape[1:])
    encoder_rows = lax.all_to_all(spread, ("zlo", "x"), 0, 0, tiled=True).reshape(-1, fw)
    encoder_own, encoder_other = over_feat(encoder_rows)

    live = (block * targets + jnp.arange(targets) >= source).astype(jnp.float32)
    total = jnp.sum(decoders[0].astype(jnp.float32) * live[:, None, None], 0).astype(jnp.bfloat16)
    earlier = [lax.ppermute(total, ("zlo", "tgt"), total_pairs(k)) for k in (3, 2, 1)]

    by_tokens = split(activations[0].T, slices)
    sliced = lax.all_to_all(by_tokens, FEAT, 0, 0, tiled=True).reshape(slices * local_feats, tokens)
    columns, pieces = select(window_ids, sliced)

    parts = [lax.ppermute(columns, ("zlo", "tgt"), window_pairs(k)) for k in (3, 2, 1)]
    target = jnp.where(zlo == block, columns, parts[0] + parts[1] + parts[2])
    swapped = lax.ppermute(target, "core", ring(CORE, 1))

    window = lax.all_to_all(pieces, ("x", "core"), 0, 0, tiled=True).reshape(X, CORE, Y * height, tokens)
    partial = gram_of(window, target, swapped).reshape(X * Y, height, fw)
    partial = lax.all_to_all(partial, ("x", "y"), 0, 0, tiled=True).reshape(X, Y, height, fw)

    pieces = prefix_of(earlier, decoders[0])
    moved = [lax.ppermute(pieces[k], "x", ring(X, k)) for k in range(1, X)]
    virtual = virtual_of([pieces[0]] + moved, encoder_own, encoder_other)
    virtual = [virtual[0]] + [lax.ppermute(virtual[k], "x", ring(X, X - k)) for k in range(1, X)]
    return weigh(partial, virtual, token_count)[None]


def solution(mesh):
    fine = Mesh(mesh.devices.reshape(ZLO, X, TGT, Y, CORE), ("zlo", "x", "tgt", "y", "core"))
    src = ("zlo", "x")
    in_specs = (
        P(src, None, FEAT),
        P(),
        P(src, "tgt", FEAT, None),
        P("tgt", src + FEAT, None),
    )
    out_specs = P(src, "tgt", FEAT, None)

    return jax.shard_map(per_device, mesh=fine, in_specs=in_specs, out_specs=out_specs, check_vma=False)
```

```python
import functools

import jax
import jax.numpy as jnp
from jax import lax
from jax.experimental import pallas as pl
from jax.experimental.pallas import tpu as pltpu
from jax.sharding import Mesh, PartitionSpec as P

ZLO, X, TGT, Y, CORE = 4, 4, 4, 4, 2
FEAT = ("y", "core")


def total_pairs(k):
    return [(z * TGT + b, z * TGT + b + k) for z in range(ZLO) for b in range(z, TGT - k)]


def window_pairs(k):
    return [(b * TGT + b, (b - k) * TGT + b) for b in range(k, TGT)]


def split_kernel(wide_ref, out_ref):
    tokens = out_ref.shape[2]
    for f in range(out_ref.shape[0]):
        out_ref[f] = wide_ref[:, f * tokens : (f + 1) * tokens]


def select_kernel(ids_ref, sliced_ref, columns_ref, pieces_ref):
    feats, tokens = sliced_ref.shape
    width = ids_ref.shape[1]
    step = 128
    wide = jnp.broadcast_to(ids_ref[pl.ds(lax.axis_index("zlo") * X + lax.axis_index("x"), 1), :], (step, width))
    columns = jnp.zeros((tokens, width), jnp.float32)
    for g in range(feats // step):
        part = sliced_ref[g * step : (g + 1) * step]
        chosen = (wide == g * step + lax.broadcasted_iota(jnp.int32, wide.shape, 0)).astype(jnp.bfloat16)
        columns += lax.dot_general(part, chosen, (((0,), (0,)), ((), ())), preferred_element_type=jnp.float32)
    columns_ref[...] = columns.astype(columns_ref.dtype)
    rows = columns.T.astype(pieces_ref.dtype)
    height = width // (Y * CORE)
    for y in range(Y):
        for c in range(CORE):
            f = y * CORE + c
            for x in range(X):
                pieces_ref[x * CORE + c, y * height : (y + 1) * height] = rows[f * height : (f + 1) * height]


def spread_kernel(rows_ref, out_ref):
    for z in range(ZLO):
        out_ref[z * X : (z + 1) * X] = rows_ref[...]


def prefix_kernel(*refs):
    total_refs, decoders_ref, out_refs = refs[: TGT - 1], refs[TGT - 1], refs[TGT:]
    step = 16
    layers = decoders_ref.shape[0]
    x = lax.axis_index("x")
    first = lax.axis_index("zlo") * X + x - lax.axis_index("tgt") * layers

    def rows(i, carry):
        at = pl.ds(i * step, step)
        base = total_refs[0][at].astype(jnp.float32)
        for ref in total_refs[1:]:
            base += ref[at].astype(jnp.float32)
        written = [decoders_ref[k, at].astype(jnp.float32) for k in range(layers - 1)]
        for r in range(X):
            layer = (x + r) % X
            out = base
            for k in range(layers - 1):
                counts = jnp.logical_and(k < layer, k >= first)
                out += written[k] * jnp.where(counts, 1.0, 0.0)
            out_refs[r][at] = out.astype(jnp.bfloat16)
        return carry

    lax.fori_loop(0, decoders_ref.shape[1] // step, rows, 0)


def virtual_kernel(*refs):
    prefix_refs, own_refs, other_ref, out_refs, rows_ref = refs[:X], refs[X : X + Y], refs[X + Y], refs[X + Y + 1 : -1], refs[-1]
    groups, slices, depth, width = rows_ref.shape
    y, core = lax.axis_index("y"), lax.axis_index("core")
    for r in range(Y):
        row = (y + Y - r) % Y
        rows_ref[:, row * CORE + core] = own_refs[r][...].reshape(groups, depth, width)
        rows_ref[:, row * CORE + 1 - core] = other_ref[r].reshape(groups, depth, width)
    height = prefix_refs[0].shape[0]
    chunk = slices * depth
    total = jnp.zeros((X * height, width), jnp.float32)
    for g in range(0, groups, 2):
        left = jnp.concatenate([ref[:, g * chunk : (g + 2) * chunk] for ref in prefix_refs], 0)
        right = rows_ref[g : g + 2].reshape(2 * chunk, width)
        total += jnp.dot(left, right, preferred_element_type=jnp.float32)
    for r in range(X):
        out_refs[r][...] = total[r * height : (r + 1) * height]


def gram_kernel(window_ref, own_ref, other_ref, out_ref):
    core = lax.axis_index("core")
    for q in range(window_ref.shape[0]):
        part = jnp.dot(window_ref[q, core], own_ref[...], preferred_element_type=jnp.float32)
        part += jnp.dot(window_ref[q, 1 - core], other_ref[...], preferred_element_type=jnp.float32)
        out_ref[q] = part.astype(out_ref.dtype)


def weigh_kernel(scale, gram_ref, *refs):
    virtual_refs, out_ref = refs[:-1], refs[-1]
    for r in range(X):
        layer = (lax.axis_index("x") + r) % X
        gram = gram_ref[layer, 0].astype(jnp.float32)
        for row in range(1, Y):
            gram += gram_ref[layer, row].astype(jnp.float32)
        out_ref[layer] = virtual_refs[r][...] * (gram * scale)


VMEM = pl.BlockSpec(memory_space=pltpu.VMEM)


def split(wide, slices):
    feats, token_count = wide.shape
    return pl.pallas_call(
        split_kernel,
        out_shape=jax.ShapeDtypeStruct((slices, feats, token_count // slices), wide.dtype),
        in_specs=[VMEM],
        out_specs=VMEM,
    )(wide)


def select(window_ids, sliced):
    tokens, width = sliced.shape[1], window_ids.shape[1]
    return pl.pallas_call(
        select_kernel,
        out_shape=(
            jax.ShapeDtypeStruct((tokens, width), jnp.bfloat16),
            jax.ShapeDtypeStruct((X * CORE, width // CORE, tokens), jnp.bfloat16),
        ),
        in_specs=[VMEM, VMEM],
        out_specs=(VMEM, VMEM),
    )(window_ids, sliced)


def spread_of(rows):
    return pl.pallas_call(
        spread_kernel,
        out_shape=jax.ShapeDtypeStruct((ZLO * rows.shape[0],) + rows.shape[1:], rows.dtype),
        in_specs=[VMEM],
        out_specs=VMEM,
    )(rows)


def prefix_of(totals, decoders):
    piece = jax.ShapeDtypeStruct(decoders.shape[1:], jnp.bfloat16)
    return pl.pallas_call(
        prefix_kernel,
        out_shape=[piece] * X,
        in_specs=[VMEM] * (len(totals) + 1),
        out_specs=[VMEM] * X,
    )(*totals, decoders)


def virtual_of(prefix, own, other):
    height, depth = prefix[0].shape
    width = other.shape[2]
    groups = ZLO * X
    return pl.pallas_call(
        virtual_kernel,
        out_shape=[jax.ShapeDtypeStruct((height, width), jnp.float32)] * X,
        in_specs=[VMEM] * (len(prefix) + len(own) + 1),
        out_specs=[VMEM] * X,
        scratch_shapes=[pltpu.VMEM((groups, Y * CORE, depth // (groups * Y * CORE), width), jnp.bfloat16)],
    )(*prefix, *own, other)


def gram_of(window, own, other):
    return pl.pallas_call(
        gram_kernel,
        out_shape=jax.ShapeDtypeStruct((X, window.shape[2], own.shape[1]), jnp.bfloat16),
        in_specs=[VMEM, VMEM, VMEM],
        out_specs=VMEM,
    )(window, own, other)


def weigh(gram, virtual, token_count):
    return pl.pallas_call(
        functools.partial(weigh_kernel, 1.0 / token_count),
        out_shape=jax.ShapeDtypeStruct((X,) + virtual[0].shape, jnp.float32),
        in_specs=[VMEM] + [VMEM] * len(virtual),
        out_specs=VMEM,
    )(gram, *virtual)


def ring(n, k):
    return [(i, (i + k) % n) for i in range(n)]


def over_feat(piece):
    others = [lax.ppermute(piece, "y", ring(Y, k)) for k in range(1, Y)]
    own = [piece] + others
    return own, lax.ppermute(jnp.stack(own), "core", ring(CORE, 1))


def per_device(activations, window_ids, decoders, encoders):
    zlo = lax.axis_index("zlo")
    block = lax.axis_index("tgt")
    x = lax.axis_index("x")
    source = zlo * X + x
    token_count, local_feats = activations.shape[1:]
    targets, height = decoders.shape[1:3]
    fw = window_ids.shape[1]
    slices = Y * CORE
    tokens = token_count // slices

    spread = spread_of(encoders)
    encoder_rows = lax.all_to_all(spread, ("zlo", "x"), 0, 0, tiled=True).reshape(-1, fw)
    encoder_own, encoder_other = over_feat(encoder_rows)

    live = (block * targets + jnp.arange(targets) >= source).astype(jnp.float32)
    total = jnp.sum(decoders[0].astype(jnp.float32) * live[:, None, None], 0).astype(jnp.bfloat16)
    earlier = [lax.ppermute(total, ("zlo", "tgt"), total_pairs(1))]
    earlier += [lax.ppermute(total, ("zlo", "tgt"), total_pairs(k)) for k in (2, 3)]

    by_tokens = split(activations[0].T, slices)
    sliced = lax.all_to_all(by_tokens, FEAT, 0, 0, tiled=True).reshape(slices * local_feats, tokens)
    columns, pieces = select(window_ids, sliced)

    parts = [lax.ppermute(columns, ("zlo", "tgt"), window_pairs(k)) for k in (3, 2, 1)]
    target = jnp.where(zlo == block, columns, parts[0] + parts[1] + parts[2])
    swapped = lax.ppermute(target, "core", ring(CORE, 1))

    window = lax.all_to_all(pieces, ("x", "core"), 0, 0, tiled=True).reshape(X, CORE, Y * height, tokens)
    partial = gram_of(window, target, swapped).reshape(X * Y, height, fw)
    partial = lax.all_to_all(partial, ("x", "y"), 0, 0, tiled=True).reshape(X, Y, height, fw)

    pieces = prefix_of(earlier, decoders[0])
    moved = [lax.ppermute(pieces[k], "x", ring(X, k)) for k in range(1, X)]
    virtual = virtual_of([pieces[0]] + moved, encoder_own, encoder_other)
    virtual = [virtual[0]] + [lax.ppermute(virtual[k], "x", ring(X, X - k)) for k in range(1, X)]
    return weigh(partial, virtual, token_count)[None]


def solution(mesh):
    fine = Mesh(mesh.devices.reshape(ZLO, X, TGT, Y, CORE), ("zlo", "x", "tgt", "y", "core"))
    src = ("zlo", "x")
    in_specs = (
        P(src, None, FEAT),
        P(),
        P(src, "tgt", FEAT, None),
        P("tgt", src + FEAT, None),
    )
    out_specs = P(src, "tgt", FEAT, None)

    return jax.shard_map(per_device, mesh=fine, in_specs=in_specs, out_specs=out_specs, check_vma=False)
```

```python
import functools

import jax
import jax.numpy as jnp
from jax import lax
from jax.experimental import pallas as pl
from jax.experimental.pallas import tpu as pltpu
from jax.sharding import Mesh, PartitionSpec as P

ZLO, X, TGT, Y, CORE = 4, 4, 4, 4, 2
FEAT = ("y", "core")


def total_pairs(k):
    return [(z * TGT + b, z * TGT + b + k) for z in range(ZLO) for b in range(z, TGT - k)]


def window_pairs(k):
    return [(b * TGT + b, (b - k) * TGT + b) for b in range(k, TGT)]


def split_kernel(wide_ref, out_ref):
    tokens = out_ref.shape[2]
    for f in range(out_ref.shape[0]):
        out_ref[f] = wide_ref[:, f * tokens : (f + 1) * tokens]


def select_kernel(ids_ref, sliced_ref, columns_ref, pieces_ref):
    feats, tokens = sliced_ref.shape
    width = ids_ref.shape[1]
    step = 128
    wide = jnp.broadcast_to(ids_ref[pl.ds(lax.axis_index("zlo") * X + lax.axis_index("x"), 1), :], (step, width))
    columns = jnp.zeros((tokens, width), jnp.float32)
    for g in range(feats // step):
        part = sliced_ref[g * step : (g + 1) * step]
        chosen = (wide == g * step + lax.broadcasted_iota(jnp.int32, wide.shape, 0)).astype(jnp.bfloat16)
        columns += lax.dot_general(part, chosen, (((0,), (0,)), ((), ())), preferred_element_type=jnp.float32)
    columns_ref[...] = columns.astype(columns_ref.dtype)
    rows = columns.T.astype(pieces_ref.dtype)
    height = width // (Y * CORE)
    for y in range(Y):
        for c in range(CORE):
            f = y * CORE + c
            for x in range(X):
                pieces_ref[x * CORE + c, y * height : (y + 1) * height] = rows[f * height : (f + 1) * height]


def prefix_kernel(*refs):
    total_refs, decoders_ref, out_refs = refs[: TGT - 1], refs[TGT - 1], refs[TGT:]
    step = 16
    layers = decoders_ref.shape[0]
    x = lax.axis_index("x")
    first = lax.axis_index("zlo") * X + x - lax.axis_index("tgt") * layers

    def rows(i, carry):
        at = pl.ds(i * step, step)
        base = total_refs[0][at].astype(jnp.float32)
        for ref in total_refs[1:]:
            base += ref[at].astype(jnp.float32)
        written = [decoders_ref[k, at].astype(jnp.float32) for k in range(layers - 1)]
        for r in range(X):
            layer = (x + r) % X
            out = base
            for k in range(layers - 1):
                counts = jnp.logical_and(k < layer, k >= first)
                out += written[k] * jnp.where(counts, 1.0, 0.0)
            out_refs[r][at] = out.astype(jnp.bfloat16)
        return carry

    lax.fori_loop(0, decoders_ref.shape[1] // step, rows, 0)


def virtual_kernel(*refs):
    prefix_refs, own_refs, other_ref, out_refs, rows_ref = refs[:X], refs[X : X + Y], refs[X + Y], refs[X + Y + 1 : -1], refs[-1]
    planes, columns, slices, depth, width = rows_ref.shape
    z, y, core = lax.axis_index("zlo"), lax.axis_index("y"), lax.axis_index("core")
    for r in range(Y):
        row = (y + Y - r) % Y
        own = own_refs[r][...].reshape(columns, planes, depth, width)
        other = other_ref[r].reshape(columns, planes, depth, width)
        for k in range(planes):
            plane = (z + planes - k) % planes
            rows_ref[plane, :, row * CORE + core] = own[:, k]
            rows_ref[plane, :, row * CORE + 1 - core] = other[:, k]
    height = prefix_refs[0].shape[0]
    chunk = columns * slices * depth // 2
    total = jnp.zeros((X * height, width), jnp.float32)
    for g in range(2 * planes):
        left = jnp.concatenate([ref[:, g * chunk : (g + 1) * chunk] for ref in prefix_refs], 0)
        half = columns // 2
        right = rows_ref[g // 2, (g % 2) * half : (g % 2 + 1) * half].reshape(chunk, width)
        total += jnp.dot(left, right, preferred_element_type=jnp.float32)
    for r in range(X):
        out_refs[r][...] = total[r * height : (r + 1) * height]


def gram_kernel(window_ref, own_ref, other_ref, out_ref):
    core = lax.axis_index("core")
    for q in range(window_ref.shape[0]):
        part = jnp.dot(window_ref[q, core], own_ref[...], preferred_element_type=jnp.float32)
        part += jnp.dot(window_ref[q, 1 - core], other_ref[...], preferred_element_type=jnp.float32)
        out_ref[q] = part.astype(out_ref.dtype)


def weigh_kernel(scale, gram_ref, *refs):
    virtual_refs, out_ref = refs[:-1], refs[-1]
    for r in range(X):
        layer = (lax.axis_index("x") + r) % X
        gram = gram_ref[layer, 0].astype(jnp.float32)
        for row in range(1, Y):
            gram += gram_ref[layer, row].astype(jnp.float32)
        out_ref[layer] = virtual_refs[r][...] * (gram * scale)


VMEM = pl.BlockSpec(memory_space=pltpu.VMEM)


def split(wide, slices):
    feats, token_count = wide.shape
    return pl.pallas_call(
        split_kernel,
        out_shape=jax.ShapeDtypeStruct((slices, feats, token_count // slices), wide.dtype),
        in_specs=[VMEM],
        out_specs=VMEM,
    )(wide)


def select(window_ids, sliced):
    tokens, width = sliced.shape[1], window_ids.shape[1]
    return pl.pallas_call(
        select_kernel,
        out_shape=(
            jax.ShapeDtypeStruct((tokens, width), jnp.bfloat16),
            jax.ShapeDtypeStruct((X * CORE, width // CORE, tokens), jnp.bfloat16),
        ),
        in_specs=[VMEM, VMEM],
        out_specs=(VMEM, VMEM),
    )(window_ids, sliced)


def prefix_of(totals, decoders):
    piece = jax.ShapeDtypeStruct(decoders.shape[1:], jnp.bfloat16)
    return pl.pallas_call(
        prefix_kernel,
        out_shape=[piece] * X,
        in_specs=[VMEM] * (len(totals) + 1),
        out_specs=[VMEM] * X,
    )(*totals, decoders)


def virtual_of(prefix, own, other):
    height, depth = prefix[0].shape
    width = other.shape[2]
    slices = Y * CORE
    return pl.pallas_call(
        virtual_kernel,
        out_shape=[jax.ShapeDtypeStruct((height, width), jnp.float32)] * X,
        in_specs=[VMEM] * (len(prefix) + len(own) + 1),
        out_specs=[VMEM] * X,
        scratch_shapes=[pltpu.VMEM((ZLO, X, slices, depth // (ZLO * X * slices), width), jnp.bfloat16)],
    )(*prefix, *own, other)


def gram_of(window, own, other):
    return pl.pallas_call(
        gram_kernel,
        out_shape=jax.ShapeDtypeStruct((X, window.shape[2], own.shape[1]), jnp.bfloat16),
        in_specs=[VMEM, VMEM, VMEM],
        out_specs=VMEM,
    )(window, own, other)


def weigh(gram, virtual, token_count):
    return pl.pallas_call(
        functools.partial(weigh_kernel, 1.0 / token_count),
        out_shape=jax.ShapeDtypeStruct((X,) + virtual[0].shape, jnp.float32),
        in_specs=[VMEM] + [VMEM] * len(virtual),
        out_specs=VMEM,
    )(gram, *virtual)


def ring(n, k):
    return [(i, (i + k) % n) for i in range(n)]


def over_feat(piece):
    others = [lax.ppermute(piece, "y", ring(Y, k)) for k in range(1, Y)]
    own = [piece] + others
    return own, lax.ppermute(jnp.stack(own), "core", ring(CORE, 1))


def per_device(activations, window_ids, decoders, encoders):
    zlo = lax.axis_index("zlo")
    block = lax.axis_index("tgt")
    x = lax.axis_index("x")
    source = zlo * X + x
    token_count, local_feats = activations.shape[1:]
    targets, height = decoders.shape[1:3]
    fw = window_ids.shape[1]
    slices = Y * CORE
    tokens = token_count // slices

    planes = [encoders] + [lax.ppermute(encoders, "zlo", ring(ZLO, k)) for k in range(1, ZLO)]
    encoder_rows = lax.all_to_all(jnp.stack(planes, 1), "x", 0, 0, tiled=True).reshape(-1, fw)
    encoder_own, encoder_other = over_feat(encoder_rows)

    live = (block * targets + jnp.arange(targets) >= source).astype(jnp.float32)
    total = jnp.sum(decoders[0].astype(jnp.float32) * live[:, None, None], 0).astype(jnp.bfloat16)
    earlier = [lax.ppermute(total, ("zlo", "tgt"), total_pairs(k)) for k in (3, 2, 1)]

    by_tokens = split(activations[0].T, slices)
    sliced = lax.all_to_all(by_tokens, FEAT, 0, 0, tiled=True).reshape(slices * local_feats, tokens)
    columns, pieces = select(window_ids, sliced)

    parts = [lax.ppermute(columns, ("zlo", "tgt"), window_pairs(k)) for k in (3, 2, 1)]
    target = jnp.where(zlo == block, columns, parts[0] + parts[1] + parts[2])
    swapped = lax.ppermute(target, "core", ring(CORE, 1))

    window = lax.all_to_all(pieces, ("x", "core"), 0, 0, tiled=True).reshape(X, CORE, Y * height, tokens)
    partial = gram_of(window, target, swapped).reshape(X * Y, height, fw)
    partial = lax.all_to_all(partial, ("x", "y"), 0, 0, tiled=True).reshape(X, Y, height, fw)

    pieces = prefix_of(earlier, decoders[0])
    moved = [lax.ppermute(pieces[k], "x", ring(X, k)) for k in range(1, X)]
    virtual = virtual_of([pieces[0]] + moved, encoder_own, encoder_other)
    virtual = [virtual[0]] + [lax.ppermute(virtual[k], "x", ring(X, X - k)) for k in range(1, X)]
    return weigh(partial, virtual, token_count)[None]


def solution(mesh):
    fine = Mesh(mesh.devices.reshape(ZLO, X, TGT, Y, CORE), ("zlo", "x", "tgt", "y", "core"))
    src = ("zlo", "x")
    in_specs = (
        P(src, None, FEAT),
        P(),
        P(src, "tgt", FEAT, None),
        P("tgt", src + FEAT, None),
    )
    out_specs = P(src, "tgt", FEAT, None)

    return jax.shard_map(per_device, mesh=fine, in_specs=in_specs, out_specs=out_specs, check_vma=False)
```

```python
import functools

import jax
import jax.numpy as jnp
from jax import lax
from jax.experimental import pallas as pl
from jax.experimental.pallas import tpu as pltpu
from jax.sharding import Mesh, PartitionSpec as P

ZLO, X, TGT, Y, CORE = 4, 4, 4, 4, 2
FEAT = ("y", "core")


def total_pairs(k):
    return [(z * TGT + b, z * TGT + b + k) for z in range(ZLO) for b in range(z, TGT - k)]


def window_pairs(k):
    return [(b * TGT + b, (b - k) * TGT + b) for b in range(k, TGT)]


def split_kernel(wide_ref, out_ref):
    tokens = out_ref.shape[2]
    for f in range(out_ref.shape[0]):
        out_ref[f] = wide_ref[:, f * tokens : (f + 1) * tokens]


def select_kernel(ids_ref, sliced_ref, columns_ref, pieces_ref):
    feats, tokens = sliced_ref.shape
    width = ids_ref.shape[1]
    step = 128
    wide = jnp.broadcast_to(ids_ref[pl.ds(lax.axis_index("zlo") * X + lax.axis_index("x"), 1), :], (step, width))
    columns = jnp.zeros((tokens, width), jnp.float32)
    for g in range(feats // step):
        part = sliced_ref[g * step : (g + 1) * step]
        chosen = (wide == g * step + lax.broadcasted_iota(jnp.int32, wide.shape, 0)).astype(jnp.bfloat16)
        columns += lax.dot_general(part, chosen, (((0,), (0,)), ((), ())), preferred_element_type=jnp.float32)
    columns_ref[...] = columns.astype(columns_ref.dtype)
    rows = columns.T.astype(pieces_ref.dtype)
    height = width // (Y * CORE)
    for y in range(Y):
        for c in range(CORE):
            f = y * CORE + c
            for x in range(X):
                pieces_ref[x * CORE + c, y * height : (y + 1) * height] = rows[f * height : (f + 1) * height]


def spread_kernel(rows_ref, out_ref):
    for z in range(ZLO):
        out_ref[z * X : (z + 1) * X] = rows_ref[...]


def prefix_kernel(*refs):
    total_refs, decoders_ref, out_refs = refs[: TGT - 1], refs[TGT - 1], refs[TGT:]
    step = 16
    layers = decoders_ref.shape[0]
    x = lax.axis_index("x")
    first = lax.axis_index("zlo") * X + x - lax.axis_index("tgt") * layers

    def rows(i, carry):
        at = pl.ds(i * step, step)
        base = total_refs[0][at].astype(jnp.float32)
        for ref in total_refs[1:]:
            base += ref[at].astype(jnp.float32)
        written = [decoders_ref[k, at].astype(jnp.float32) for k in range(layers - 1)]
        for r in range(X):
            layer = (x + r) % X
            out = base
            for k in range(layers - 1):
                counts = jnp.logical_and(k < layer, k >= first)
                out += written[k] * jnp.where(counts, 1.0, 0.0)
            out_refs[r][at] = out.astype(jnp.bfloat16)
        return carry

    lax.fori_loop(0, decoders_ref.shape[1] // step, rows, 0)


def virtual_kernel(*refs):
    prefix_refs, own_refs, other_ref, out_refs, rows_ref = refs[:X], refs[X : X + Y], refs[X + Y], refs[X + Y + 1 : -1], refs[-1]
    groups, slices, depth, width = rows_ref.shape
    y, core = lax.axis_index("y"), lax.axis_index("core")
    for r in range(Y):
        row = (y + Y - r) % Y
        rows_ref[:, row * CORE + core] = own_refs[r][...].reshape(groups, depth, width)
        rows_ref[:, row * CORE + 1 - core] = other_ref[r].reshape(groups, depth, width)
    height = prefix_refs[0].shape[0]
    chunk = slices * depth
    total = jnp.zeros((X * height, width), jnp.float32)
    for g in range(0, groups, 2):
        left = jnp.concatenate([ref[:, g * chunk : (g + 2) * chunk] for ref in prefix_refs], 0)
        right = rows_ref[g : g + 2].reshape(2 * chunk, width)
        total += jnp.dot(left, right, preferred_element_type=jnp.float32)
    for r in range(X):
        out_refs[r][...] = total[r * height : (r + 1) * height]


def gram_kernel(window_ref, own_ref, other_ref, out_ref):
    core = lax.axis_index("core")
    for q in range(window_ref.shape[0]):
        part = jnp.dot(window_ref[q, core], own_ref[...], preferred_element_type=jnp.float32)
        part += jnp.dot(window_ref[q, 1 - core], other_ref[...], preferred_element_type=jnp.float32)
        out_ref[q] = part.astype(out_ref.dtype)


def add_kernel(scale, gram_ref, out_ref):
    for layer in range(gram_ref.shape[0]):
        gram = gram_ref[layer, 0].astype(jnp.float32)
        for row in range(1, gram_ref.shape[1]):
            gram += gram_ref[layer, row].astype(jnp.float32)
        out_ref[layer] = gram * scale


def weigh_kernel(gram_ref, *refs):
    virtual_refs, out_ref = refs[:-1], refs[-1]
    for r in range(X):
        layer = (lax.axis_index("x") + r) % X
        out_ref[layer] = virtual_refs[r][...] * gram_ref[layer]


VMEM = pl.BlockSpec(memory_space=pltpu.VMEM)


def split(wide, slices):
    feats, token_count = wide.shape
    return pl.pallas_call(
        split_kernel,
        out_shape=jax.ShapeDtypeStruct((slices, feats, token_count // slices), wide.dtype),
        in_specs=[VMEM],
        out_specs=VMEM,
    )(wide)


def select(window_ids, sliced):
    tokens, width = sliced.shape[1], window_ids.shape[1]
    return pl.pallas_call(
        select_kernel,
        out_shape=(
            jax.ShapeDtypeStruct((tokens, width), jnp.bfloat16),
            jax.ShapeDtypeStruct((X * CORE, width // CORE, tokens), jnp.bfloat16),
        ),
        in_specs=[VMEM, VMEM],
        out_specs=(VMEM, VMEM),
    )(window_ids, sliced)


def spread_of(rows):
    return pl.pallas_call(
        spread_kernel,
        out_shape=jax.ShapeDtypeStruct((ZLO * rows.shape[0],) + rows.shape[1:], rows.dtype),
        in_specs=[VMEM],
        out_specs=VMEM,
    )(rows)


def prefix_of(totals, decoders):
    piece = jax.ShapeDtypeStruct(decoders.shape[1:], jnp.bfloat16)
    return pl.pallas_call(
        prefix_kernel,
        out_shape=[piece] * X,
        in_specs=[VMEM] * (len(totals) + 1),
        out_specs=[VMEM] * X,
    )(*totals, decoders)


def virtual_of(prefix, own, other):
    height, depth = prefix[0].shape
    width = other.shape[2]
    groups = ZLO * X
    return pl.pallas_call(
        virtual_kernel,
        out_shape=[jax.ShapeDtypeStruct((height, width), jnp.float32)] * X,
        in_specs=[VMEM] * (len(prefix) + len(own) + 1),
        out_specs=[VMEM] * X,
        scratch_shapes=[pltpu.VMEM((groups, Y * CORE, depth // (groups * Y * CORE), width), jnp.bfloat16)],
    )(*prefix, *own, other)


def gram_of(window, own, other):
    return pl.pallas_call(
        gram_kernel,
        out_shape=jax.ShapeDtypeStruct((X, window.shape[2], own.shape[1]), jnp.bfloat16),
        in_specs=[VMEM, VMEM, VMEM],
        out_specs=VMEM,
    )(window, own, other)


def added(gram, token_count):
    layers, _, height, width = gram.shape
    return pl.pallas_call(
        functools.partial(add_kernel, 1.0 / token_count),
        out_shape=jax.ShapeDtypeStruct((layers, height, width), jnp.float32),
        in_specs=[VMEM],
        out_specs=VMEM,
    )(gram)


def weigh(gram, virtual):
    return pl.pallas_call(
        weigh_kernel,
        out_shape=jax.ShapeDtypeStruct(gram.shape, jnp.float32),
        in_specs=[VMEM] * (len(virtual) + 1),
        out_specs=VMEM,
    )(gram, *virtual)


def ring(n, k):
    return [(i, (i + k) % n) for i in range(n)]


def over_feat(piece):
    others = [lax.ppermute(piece, "y", ring(Y, k)) for k in range(1, Y)]
    own = [piece] + others
    return own, lax.ppermute(jnp.stack(own), "core", ring(CORE, 1))


def per_device(activations, window_ids, decoders, encoders):
    zlo = lax.axis_index("zlo")
    block = lax.axis_index("tgt")
    x = lax.axis_index("x")
    source = zlo * X + x
    token_count, local_feats = activations.shape[1:]
    targets, height = decoders.shape[1:3]
    fw = window_ids.shape[1]
    slices = Y * CORE
    tokens = token_count // slices

    spread = spread_of(encoders)
    encoder_rows = lax.all_to_all(spread, ("zlo", "x"), 0, 0, tiled=True).reshape(-1, fw)
    encoder_own, encoder_other = over_feat(encoder_rows)

    live = (block * targets + jnp.arange(targets) >= source).astype(jnp.float32)
    total = jnp.sum(decoders[0].astype(jnp.float32) * live[:, None, None], 0).astype(jnp.bfloat16)
    earlier = [lax.ppermute(total, ("zlo", "tgt"), total_pairs(1))]
    earlier += [lax.ppermute(total, ("zlo", "tgt"), total_pairs(k)) for k in (2, 3)]

    by_tokens = split(activations[0].T, slices)
    sliced = lax.all_to_all(by_tokens, FEAT, 0, 0, tiled=True).reshape(slices * local_feats, tokens)
    columns, pieces = select(window_ids, sliced)

    parts = [lax.ppermute(columns, ("zlo", "tgt"), window_pairs(k)) for k in (3, 2, 1)]
    target = jnp.where(zlo == block, columns, parts[0] + parts[1] + parts[2])
    swapped = lax.ppermute(target, "core", ring(CORE, 1))

    window = lax.all_to_all(pieces, ("x", "core"), 0, 0, tiled=True).reshape(X, CORE, Y * height, tokens)
    partial = gram_of(window, target, swapped).reshape(X * Y, height, fw)
    partial = lax.all_to_all(partial, ("x", "y"), 0, 0, tiled=True).reshape(X, Y, height, fw)

    pieces = prefix_of(earlier, decoders[0])
    moved = [lax.ppermute(pieces[k], "x", ring(X, k)) for k in range(1, X - 1)]
    moved.append(lax.ppermute(pieces[X - 1], "x", ring(X, X - 1)))
    virtual = virtual_of([pieces[0]] + moved, encoder_own, encoder_other)
    virtual = [virtual[0]] + [lax.ppermute(virtual[k], "x", ring(X, X - k)) for k in range(1, X)]
    gram = added(partial, token_count)
    return weigh(gram, virtual)[None]


def solution(mesh):
    fine = Mesh(mesh.devices.reshape(ZLO, X, TGT, Y, CORE), ("zlo", "x", "tgt", "y", "core"))
    src = ("zlo", "x")
    in_specs = (
        P(src, None, FEAT),
        P(),
        P(src, "tgt", FEAT, None),
        P("tgt", src + FEAT, None),
    )
    out_specs = P(src, "tgt", FEAT, None)

    return jax.shard_map(per_device, mesh=fine, in_specs=in_specs, out_specs=out_specs, check_vma=False)
```

```python
import functools

import jax
import jax.numpy as jnp
from jax import lax
from jax.experimental import pallas as pl
from jax.experimental.pallas import tpu as pltpu
from jax.sharding import Mesh, PartitionSpec as P

ZLO, X, TGT, Y, CORE = 4, 4, 4, 4, 2
FEAT = ("y", "core")


def total_pairs(k):
    return [(z * TGT + b, z * TGT + b + k) for z in range(ZLO) for b in range(z, TGT - k)]


def window_pairs(k):
    return [(b * TGT + b, (b - k) * TGT + b) for b in range(k, TGT)]


def split_kernel(wide_ref, out_ref):
    tokens = out_ref.shape[2]
    for f in range(out_ref.shape[0]):
        out_ref[f] = wide_ref[:, f * tokens : (f + 1) * tokens]


def select_kernel(ids_ref, sliced_ref, columns_ref, pieces_ref):
    feats, tokens = sliced_ref.shape
    width = ids_ref.shape[1]
    step = 128
    wide = jnp.broadcast_to(ids_ref[pl.ds(lax.axis_index("zlo") * X + lax.axis_index("x"), 1), :], (step, width))
    columns = jnp.zeros((tokens, width), jnp.float32)
    for g in range(feats // step):
        part = sliced_ref[g * step : (g + 1) * step]
        chosen = (wide == g * step + lax.broadcasted_iota(jnp.int32, wide.shape, 0)).astype(jnp.bfloat16)
        columns += lax.dot_general(part, chosen, (((0,), (0,)), ((), ())), preferred_element_type=jnp.float32)
    columns_ref[...] = columns.astype(columns_ref.dtype)
    rows = columns.T.astype(pieces_ref.dtype)
    height = width // (Y * CORE)
    for y in range(Y):
        for c in range(CORE):
            f = y * CORE + c
            for x in range(X):
                pieces_ref[x * CORE + c, y * height : (y + 1) * height] = rows[f * height : (f + 1) * height]


def spread_kernel(rows_ref, out_ref):
    for z in range(ZLO):
        out_ref[z * X : (z + 1) * X] = rows_ref[...]


def prefix_kernel(*refs):
    total_refs, decoders_ref, out_refs = refs[: TGT - 1], refs[TGT - 1], refs[TGT:]
    step = 16
    layers = decoders_ref.shape[0]
    x = lax.axis_index("x")
    first = lax.axis_index("zlo") * X + x - lax.axis_index("tgt") * layers

    def rows(i, carry):
        at = pl.ds(i * step, step)
        base = total_refs[0][at].astype(jnp.float32)
        for ref in total_refs[1:]:
            base += ref[at].astype(jnp.float32)
        written = [decoders_ref[k, at].astype(jnp.float32) for k in range(layers - 1)]
        for r in range(X):
            layer = (x + r) % X
            out = base
            for k in range(layers - 1):
                counts = jnp.logical_and(k < layer, k >= first)
                out += written[k] * jnp.where(counts, 1.0, 0.0)
            out_refs[r][at] = out.astype(jnp.bfloat16)
        return carry

    lax.fori_loop(0, decoders_ref.shape[1] // step, rows, 0)


def virtual_kernel(*refs):
    prefix_refs, own_refs, other_ref, out_refs, rows_ref = refs[:X], refs[X : X + Y], refs[X + Y], refs[X + Y + 1 : -1], refs[-1]
    groups, slices, depth, width = rows_ref.shape
    y, core = lax.axis_index("y"), lax.axis_index("core")
    for r in range(Y):
        row = (y + Y - r) % Y
        rows_ref[:, row * CORE + core] = own_refs[r][...].reshape(groups, depth, width)
        rows_ref[:, row * CORE + 1 - core] = other_ref[r].reshape(groups, depth, width)
    height = prefix_refs[0].shape[0]
    chunk = slices * depth
    total = jnp.zeros((X * height, width), jnp.float32)
    for g in range(0, groups, 2):
        left = jnp.concatenate([ref[:, g * chunk : (g + 2) * chunk] for ref in prefix_refs], 0)
        right = rows_ref[g : g + 2].reshape(2 * chunk, width)
        total += jnp.dot(left, right, preferred_element_type=jnp.float32)
    for r in range(X):
        out_refs[r][...] = total[r * height : (r + 1) * height]


def gram_kernel(window_ref, own_ref, other_ref, out_ref):
    core = lax.axis_index("core")
    for q in range(window_ref.shape[0]):
        part = jnp.dot(window_ref[q, core], own_ref[...], preferred_element_type=jnp.float32)
        part += jnp.dot(window_ref[q, 1 - core], other_ref[...], preferred_element_type=jnp.float32)
        out_ref[q] = part.astype(out_ref.dtype)


def add_kernel(scale, gram_ref, out_ref):
    for layer in range(gram_ref.shape[0]):
        gram = gram_ref[layer, 0].astype(jnp.float32)
        for row in range(1, gram_ref.shape[1]):
            gram += gram_ref[layer, row].astype(jnp.float32)
        out_ref[layer] = gram * scale


def weigh_kernel(gram_ref, *refs):
    virtual_refs, out_ref = refs[:-1], refs[-1]
    for r in range(X):
        layer = (lax.axis_index("x") + r) % X
        out_ref[layer] = virtual_refs[r][...] * gram_ref[layer]


VMEM = pl.BlockSpec(memory_space=pltpu.VMEM)


def split(wide, slices):
    feats, token_count = wide.shape
    return pl.pallas_call(
        split_kernel,
        out_shape=jax.ShapeDtypeStruct((slices, feats, token_count // slices), wide.dtype),
        in_specs=[VMEM],
        out_specs=VMEM,
    )(wide)


def select(window_ids, sliced):
    tokens, width = sliced.shape[1], window_ids.shape[1]
    return pl.pallas_call(
        select_kernel,
        out_shape=(
            jax.ShapeDtypeStruct((tokens, width), jnp.bfloat16),
            jax.ShapeDtypeStruct((X * CORE, width // CORE, tokens), jnp.bfloat16),
        ),
        in_specs=[VMEM, VMEM],
        out_specs=(VMEM, VMEM),
    )(window_ids, sliced)


def spread_of(rows):
    return pl.pallas_call(
        spread_kernel,
        out_shape=jax.ShapeDtypeStruct((ZLO * rows.shape[0],) + rows.shape[1:], rows.dtype),
        in_specs=[VMEM],
        out_specs=VMEM,
    )(rows)


def prefix_of(totals, decoders):
    piece = jax.ShapeDtypeStruct(decoders.shape[1:], jnp.bfloat16)
    return pl.pallas_call(
        prefix_kernel,
        out_shape=[piece] * X,
        in_specs=[VMEM] * (len(totals) + 1),
        out_specs=[VMEM] * X,
    )(*totals, decoders)


def virtual_of(prefix, own, other):
    height, depth = prefix[0].shape
    width = other.shape[2]
    groups = ZLO * X
    return pl.pallas_call(
        virtual_kernel,
        out_shape=[jax.ShapeDtypeStruct((height, width), jnp.float32)] * X,
        in_specs=[VMEM] * (len(prefix) + len(own) + 1),
        out_specs=[VMEM] * X,
        scratch_shapes=[pltpu.VMEM((groups, Y * CORE, depth // (groups * Y * CORE), width), jnp.bfloat16)],
    )(*prefix, *own, other)


def gram_of(window, own, other):
    return pl.pallas_call(
        gram_kernel,
        out_shape=jax.ShapeDtypeStruct((X, window.shape[2], own.shape[1]), jnp.bfloat16),
        in_specs=[VMEM, VMEM, VMEM],
        out_specs=VMEM,
    )(window, own, other)


def added(gram, token_count):
    layers, _, height, width = gram.shape
    return pl.pallas_call(
        functools.partial(add_kernel, 1.0 / token_count),
        out_shape=jax.ShapeDtypeStruct((layers, height, width), jnp.float32),
        in_specs=[VMEM],
        out_specs=VMEM,
    )(gram)


def weigh(gram, virtual):
    return pl.pallas_call(
        weigh_kernel,
        out_shape=jax.ShapeDtypeStruct(gram.shape, jnp.float32),
        in_specs=[VMEM] * (len(virtual) + 1),
        out_specs=VMEM,
    )(gram, *virtual)


def ring(n, k):
    return [(i, (i + k) % n) for i in range(n)]


def over_feat(piece):
    others = [lax.ppermute(piece, "y", ring(Y, k)) for k in range(1, Y)]
    own = [piece] + others
    return own, lax.ppermute(jnp.stack(own), "core", ring(CORE, 1))


def per_device(activations, window_ids, decoders, encoders):
    zlo = lax.axis_index("zlo")
    block = lax.axis_index("tgt")
    x = lax.axis_index("x")
    source = zlo * X + x
    token_count, local_feats = activations.shape[1:]
    targets, height = decoders.shape[1:3]
    fw = window_ids.shape[1]
    slices = Y * CORE
    tokens = token_count // slices

    spread = spread_of(encoders)
    encoder_rows = lax.all_to_all(spread, ("zlo", "x"), 0, 0, tiled=True).reshape(-1, fw)
    encoder_own, encoder_other = over_feat(encoder_rows)

    live = (block * targets + jnp.arange(targets) >= source).astype(jnp.float32)
    total = jnp.sum(decoders[0].astype(jnp.float32) * live[:, None, None], 0).astype(jnp.bfloat16)
    earlier = [lax.ppermute(total, ("zlo", "tgt"), total_pairs(1))]
    earlier += [lax.ppermute(total, ("zlo", "tgt"), total_pairs(k)) for k in (2, 3)]

    by_tokens = split(activations[0].T, slices)
    sliced = lax.all_to_all(by_tokens, FEAT, 0, 0, tiled=True).reshape(slices * local_feats, tokens)
    columns, pieces = select(window_ids, sliced)

    parts = [lax.ppermute(columns, ("zlo", "tgt"), window_pairs(k)) for k in (3, 2, 1)]
    target = jnp.where(zlo == block, columns, parts[0] + parts[1] + parts[2])
    swapped = lax.ppermute(target, "core", ring(CORE, 1))

    window = lax.all_to_all(pieces, ("x", "core"), 0, 0, tiled=True).reshape(X, CORE, Y * height, tokens)
    partial = gram_of(window, target, swapped).reshape(X * Y, height, fw)
    partial = lax.all_to_all(partial, ("x", "y"), 0, 0, tiled=True).reshape(X, Y, height, fw)

    pieces = prefix_of(earlier, decoders[0])
    moved = [lax.ppermute(pieces[k], "x", ring(X, k)) for k in range(1, X)]
    virtual = virtual_of([pieces[0]] + moved, encoder_own, encoder_other)
    far = lax.ppermute(virtual[2], "x", ring(X, X - 2))
    near = [lax.ppermute(virtual[k], "x", ring(X, X - k)) for k in (1, 3)]
    virtual = [virtual[0], near[0], far, near[1]]
    gram = added(partial, token_count)
    return weigh(gram, virtual)[None]


def solution(mesh):
    fine = Mesh(mesh.devices.reshape(ZLO, X, TGT, Y, CORE), ("zlo", "x", "tgt", "y", "core"))
    src = ("zlo", "x")
    in_specs = (
        P(src, None, FEAT),
        P(),
        P(src, "tgt", FEAT, None),
        P("tgt", src + FEAT, None),
    )
    out_specs = P(src, "tgt", FEAT, None)

    return jax.shard_map(per_device, mesh=fine, in_specs=in_specs, out_specs=out_specs, check_vma=False)
```
